32 devices in a mesh: section: 4 (over z), ctx: 8 (over y, x, core).
Axes of the slice: x: 2, y: 2, z: 4, core: 2. Of those that a mesh axis runs over, the one named last changes fastest.
Arguments:
- stream: bfloat16 [1024, 2688], P('ctx'), may hold values from -6 to 6
- queries: bfloat16 [4, 1024, 2048], P('section', 'ctx'), may hold values from -51 to 51
- keys: bfloat16 [4, 1024, 1024], P('section', 'ctx'), may hold values from -4 to 4
- values: bfloat16 [4, 1024, 1024], P('section', 'ctx'), may hold values from -120 to 120
- out_weight: bfloat16 [4, 2048, 2688], P('section', 'ctx'), may hold values from -0.125 to 0.125
- gains: bfloat16 [4, 2688], P('section'), may hold values from 0.099609375 to 1.8984375
Outputs:
- layer_outputs: bfloat16 [4, 1024, 2688], P('section', 'ctx')
The draws below stay inside these ranges and needn't reach their ends.
All inputs are finite; a program needn't handle non-finite values.
Results may differ from the reference program's by a relative error of at most 0.009.
Values may be sent and summed in bfloat16 or wider, within the bound.
A program may use at most 64 MiB of HBM per device.

```python
import math
import jax
import jax.numpy as jnp
from jax import lax

HQ = 16
KEY_HEADS = 8
HEAD_WIDTH = 128
STREAM_WIDTH = 2688
WINDOW_LENGTH = 1024
QUERY_SCALAR = 168
LAYER_COUNT = 4
TOKEN_COUNT = 1024
QUERY_PER_KEY = 2


def draw_pair(key):
    keys_shape_tuple = (LAYER_COUNT, TOKEN_COUNT, KEY_HEADS * HEAD_WIDTH)
    queries_shape_tuple = (LAYER_COUNT, TOKEN_COUNT, HQ * HEAD_WIDTH)
    sampled_keys = jax.random.truncated_normal(jax.random.fold_in(key, 11), -4.0, 4.0, keys_shape_tuple, jnp.float32)
    drawn_queries = jax.random.truncated_normal(jax.random.fold_in(key, 12), -4.0, 4.0, queries_shape_tuple, jnp.float32)
    return (drawn_queries, sampled_keys)


def draw_queries(key, part):
    return draw_pair(key)[0].astype(jnp.bfloat16)


def draw_keys(key, part):
    return draw_pair(key)[1].astype(jnp.bfloat16)


def draw_values(key, part):
    value_shape_tuple = (LAYER_COUNT, TOKEN_COUNT, KEY_HEADS * HEAD_WIDTH)
    base_draw = jax.random.truncated_normal(jax.random.fold_in(key, 21), -4.0, 4.0, value_shape_tuple, jnp.float32)
    return base_draw.astype(jnp.bfloat16)


def levels(key, dims, shards, smallest, high):
    level = 1.0
    for axis_at, parts in shards:
        heights = jax.random.uniform(jax.random.fold_in(jax.random.fold_in(key, 6), axis_at), (parts,), jnp.float32, smallest / len(shards), high / len(shards))
        level = level * jnp.repeat(jnp.exp(heights), dims[axis_at] // parts).reshape((-1,) + (1,) * (len(dims) - 1 - axis_at))
    return level


def bell_draw(key, shape, width, limit, pieces=(), kind=jnp.bfloat16):
    loudness = levels(key, shape, pieces, -0.22, 0.18) if pieces else 1.0
    array = jax.random.normal(key, shape, jnp.float32) * width * loudness
    return jnp.minimum(jnp.maximum(array, -limit), limit).astype(kind)


def setup_inputs(seed: int = 0) -> dict:
    seeds = jax.random.split(jax.random.key(seed), 7)
    stream = bell_draw(seeds[0], (TOKEN_COUNT, STREAM_WIDTH), 1.0, 6.0, ((0, 8),))
    queries = draw_queries(jax.random.fold_in(seeds[6], 71), 0)
    keys = draw_keys(jax.random.fold_in(seeds[6], 71), 0)
    values = draw_values(jax.random.fold_in(seeds[6], 71), 0)
    out_weight = bell_draw(seeds[4], (LAYER_COUNT, HQ * HEAD_WIDTH, STREAM_WIDTH), (HQ * HEAD_WIDTH) ** -0.5, 0.125, ((0, 4), (1, 8)))
    gains = jnp.clip(1.0 + 0.18 * jax.random.normal(seeds[5], (LAYER_COUNT, STREAM_WIDTH), jnp.float32), 0.099609375, 1.8984375).astype(jnp.bfloat16)
    return dict(stream=stream, queries=queries, keys=keys, values=values, out_weight=out_weight, gains=gains)


norm_eps = 1e-06

def attend_block(query_matrix_rows, key_matrix_rows, value_matrix_rows, allowed, scale_factor):
    scores = jnp.einsum('qhgd,khd->hgqk', query_matrix_rows.astype(jnp.float32), key_matrix_rows.astype(jnp.float32)) * scale_factor
    scores = jnp.where(allowed, scores, -jnp.inf)
    row_top = lax.optimization_barrier(jnp.max(scores, axis=-1, keepdims=True))
    exponent = jnp.exp(scores - row_top)
    row_total = lax.optimization_barrier(jnp.sum(exponent, axis=-1, keepdims=True))
    weights = lax.optimization_barrier(exponent.astype(jnp.bfloat16)).astype(jnp.float32)
    mixed_rows = jnp.einsum('hgqk,khd->qhgd', weights, value_matrix_rows.astype(jnp.float32))
    return mixed_rows / jnp.transpose(row_total, (2, 0, 1, 3))

def attend_layer(queries, keys, values, weight_matrix, gain_row):
    rows_per_block = math.gcd(TOKEN_COUNT, 512)
    block_count = TOKEN_COUNT // rows_per_block
    scale_factor = QUERY_SCALAR ** (-0.5)
    empty_padding_rows = jnp.zeros((WINDOW_LENGTH, KEY_HEADS * HEAD_WIDTH), keys.dtype)
    keys_with_padding = jnp.concatenate([empty_padding_rows, keys], axis=0)
    values_with_padding = jnp.concatenate([empty_padding_rows, values], axis=0)

    def one_block(block_index):
        leading_row = block_index * rows_per_block
        query_matrix_rows = lax.dynamic_slice_in_dim(queries, leading_row, rows_per_block, 0).reshape(rows_per_block, KEY_HEADS, QUERY_PER_KEY, HEAD_WIDTH)
        key_matrix_rows = lax.dynamic_slice_in_dim(keys_with_padding, leading_row, rows_per_block + WINDOW_LENGTH, 0).reshape(rows_per_block + WINDOW_LENGTH, KEY_HEADS, HEAD_WIDTH)
        value_matrix_rows = lax.dynamic_slice_in_dim(values_with_padding, leading_row, rows_per_block + WINDOW_LENGTH, 0).reshape(rows_per_block + WINDOW_LENGTH, KEY_HEADS, HEAD_WIDTH)
        query_pos = leading_row + jnp.arange(rows_per_block, dtype=jnp.int32)
        key_pos = leading_row - WINDOW_LENGTH + jnp.arange(rows_per_block + WINDOW_LENGTH, dtype=jnp.int32)
        allowed = (key_pos[None, :] >= 0) & (key_pos[None, :] <= query_pos[:, None]) & (key_pos[None, :] > query_pos[:, None] - WINDOW_LENGTH)
        mixed_rows = attend_block(query_matrix_rows, key_matrix_rows, value_matrix_rows, allowed, scale_factor)
        attended = mixed_rows.reshape(rows_per_block, HQ * HEAD_WIDTH).astype(jnp.bfloat16)
        return jnp.dot(attended, weight_matrix, preferred_element_type=jnp.float32)
    projected = lax.map(one_block, jnp.arange(block_count, dtype=jnp.int32)).reshape(TOKEN_COUNT, STREAM_WIDTH)
    mean_square = lax.optimization_barrier(jnp.mean(projected * projected, axis=-1, keepdims=True))
    return projected * lax.rsqrt(mean_square + norm_eps) * gain_row.astype(jnp.float32)

def reference(stream, queries, keys, values, out_weight, gains):
    running = stream.astype(jnp.float32)
    outputs_list = []
    for layer_index in range(LAYER_COUNT):
        branch = attend_layer(queries[layer_index], keys[layer_index], values[layer_index], out_weight[layer_index], gains[layer_index])
        running = running + branch
        outputs_list.append(running.astype(jnp.bfloat16))
    return jnp.stack(outputs_list)
```

```python
import functools
import math

import jax
import jax.numpy as jnp
from jax import lax
from jax.experimental import pallas as pl
from jax.experimental.pallas import tpu as pltpu
from jax.sharding import PartitionSpec as P

KEY_HEADS = 8
HEAD_WIDTH = 128
WINDOW_LENGTH = 1024
QUERY_SCALAR = 168
QUERY_PER_KEY = 2


norm_eps = 1e-06


def passed_along(block, axis, distance):
    devices = range(lax.axis_size(axis))
    route = [(i - distance, i) for i in devices if i - distance in devices]
    return lax.ppermute(block, axis, route)


def attend_block(query_matrix_rows, key_matrix_rows, value_matrix_rows, allowed, scale_factor):
    scores = (
        jnp.einsum(
            "qhgd,khd->hgqk", query_matrix_rows, key_matrix_rows, preferred_element_type=jnp.float32
        )
        * scale_factor
    )
    scores = jnp.where(allowed, scores, -jnp.inf)
    row_top = jnp.max(scores, axis=-1, keepdims=True)
    exponent = jnp.exp(scores - row_top)
    row_total = jnp.sum(exponent, axis=-1, keepdims=True)
    weights = exponent.astype(jnp.bfloat16)
    mixed_rows = jnp.einsum(
        "hgqk,khd->qhgd", weights, value_matrix_rows, preferred_element_type=jnp.float32
    )
    return mixed_rows / jnp.transpose(row_total, (2, 0, 1, 3))


def local(stream, queries, keys, values, out_weight, gains):
    tok_rows = stream.shape[0]
    span_rows = min(tok_rows, WINDOW_LENGTH)
    hop_count = WINDOW_LENGTH // span_rows
    own_tail = (keys[0, tok_rows - span_rows :], values[0, tok_rows - span_rows :])
    pieces = [
        passed_along((own_tail[0], own_tail[1]), "ctx", distance)
        for distance in range(hop_count, 0, -1)
    ]
    key_matrix_rows = jnp.concatenate([piece_pair[0] for piece_pair in pieces] + [keys[0]], axis=0)
    value_matrix_rows = jnp.concatenate(
        [piece_pair[1] for piece_pair in pieces] + [values[0]], axis=0
    )
    ctx_base = lax.axis_index("ctx") * tok_rows
    query_pos = ctx_base + jnp.arange(tok_rows, dtype=jnp.int32)
    key_pos = ctx_base - WINDOW_LENGTH + jnp.arange(WINDOW_LENGTH + tok_rows, dtype=jnp.int32)
    allowed = (
        (key_pos[None, :] >= 0)
        & (key_pos[None, :] <= query_pos[:, None])
        & (key_pos[None, :] > query_pos[:, None] - WINDOW_LENGTH)
    )
    scale_factor = QUERY_SCALAR ** (-0.5)
    heads_per_block = math.gcd(KEY_HEADS, 4)
    query_width = heads_per_block * QUERY_PER_KEY * HEAD_WIDTH
    key_width = heads_per_block * HEAD_WIDTH
    outputs_list = []
    for query_head_group in range(KEY_HEADS // heads_per_block):
        query_cols = queries[
            0, :, query_head_group * query_width : (query_head_group + 1) * query_width
        ].reshape(tok_rows, heads_per_block, QUERY_PER_KEY, HEAD_WIDTH)
        key_cols = key_matrix_rows[
            :, query_head_group * key_width : (query_head_group + 1) * key_width
        ].reshape(WINDOW_LENGTH + tok_rows, heads_per_block, HEAD_WIDTH)
        value_cols = value_matrix_rows[
            :, query_head_group * key_width : (query_head_group + 1) * key_width
        ].reshape(WINDOW_LENGTH + tok_rows, heads_per_block, HEAD_WIDTH)
        mixed_rows = attend_block(query_cols, key_cols, value_cols, allowed, scale_factor)
        outputs_list.append(mixed_rows.reshape(tok_rows, query_width))
    attended = jnp.concatenate(outputs_list, axis=1).astype(jnp.bfloat16)
    projected = jnp.dot(
        attended,
        lax.all_gather(out_weight[0], "ctx", axis=0, tiled=True),
        preferred_element_type=jnp.float32,
    )
    mean_square = jnp.mean(projected * projected, axis=-1, keepdims=True)
    branch = projected * lax.rsqrt(mean_square + norm_eps) * gains[0].astype(jnp.float32)
    section_index = lax.axis_index("section")
    section_count = lax.axis_size("section")
    running = jnp.where(
        section_index == 0, stream.astype(jnp.float32) + branch, jnp.zeros_like(branch)
    )
    for turn_index in range(section_count - 1):
        arrived = passed_along(running.astype(jnp.bfloat16), "section", 1).astype(running.dtype)
        running = jnp.where(section_index == turn_index + 1, arrived + branch, running)
    return running.astype(jnp.bfloat16)[None]


LANES = 128
MESH = pl.DeviceIdType.MESH
CHUNKS = 8
PIECES = 2
FIRST = 2
SECOND = 5
LAST = 8
HOP = 2
TILE = 512
VMEM_GRANT = 60_000_000


def column_tiles(start, stop, width):
    return [(at, min(at + width, stop) - at) for at in range(start, stop, width)]


def fused_kernel(
    sections,
    chunks,
    pieces,
    half,
    gains_hbm,
    stream_ref,
    q_ref,
    k_ref,
    v_ref,
    w_hbm,
    out_ref,
    qbuf,
    kbuf,
    vbuf,
    vturned,
    w_ref,
    gains_ref,
    att,
    pair_out,
    pair_in,
    x1_out,
    y1_out,
    first_in,
    x2_out,
    y2_out,
    second_in,
    own,
    keep_me,
    keep_x,
    keep_y,
    base,
    local_sem,
    key_sem,
    value_sem,
    query_sem,
    sent_sem,
    pair_sem,
    first_sem,
    second_sem,
    chain_sem,
):
    me = lax.axis_index("ctx")
    section = lax.axis_index("section")
    devices, chunk_rows, query_width = qbuf.shape[1:]
    width = w_ref.shape[1]
    rows = chunks * chunk_rows
    piece_rows = chunk_rows // pieces
    quarter, pair_count = devices // 4, devices // 2
    core = me % 2
    across = (me // quarter) % 2
    up = me // pair_count
    flips = (1 - 2 * core, quarter * (1 - 2 * across), pair_count * (1 - 2 * up))

    def peer(flip_core, flip_x, flip_y):
        return me + flips[0] * flip_core + flips[1] * flip_x + flips[2] * flip_y

    sibling, beside, above, diagonal = peer(1, 0, 0), peer(0, 1, 0), peer(0, 0, 1), peer(0, 1, 1)
    has_prev = jnp.minimum(section, 1)
    has_next = jnp.minimum(sections - 1 - section, 1)

    def own_rows(buf):
        return buf.at[pl.ds(pl.multiple_of(me * rows, rows), rows)]

    def head_columns(ref, who, span):
        return ref.at[:, pl.ds(pl.multiple_of(who * span, span), span)]

    w_copy = pltpu.make_async_copy(w_hbm, w_ref, local_sem.at[0])
    w_copy.start()
    gains_copy = pltpu.make_async_copy(gains_hbm, gains_ref, local_sem.at[1])
    gains_copy.start()

    @pl.when(section == 0)
    def _():
        for piece in range(chunks * pieces):
            pltpu.make_async_copy(
                stream_ref.at[pl.ds(piece * piece_rows, piece_rows)],
                base.at[piece],
                chain_sem.at[piece],
            ).start()

    def query_part(who, chunk):
        source = q_ref.at[
            pl.ds(chunk * chunk_rows, chunk_rows),
            pl.ds(pl.multiple_of(who * query_width, query_width), query_width),
        ]
        return source, qbuf.at[chunk, me], sent_sem.at[2], query_sem.at[chunk]

    def blocks_for(who):
        key_block = head_columns(k_ref, who, HEAD_WIDTH), own_rows(kbuf), sent_sem.at[0], key_sem
        value_block = (
            head_columns(v_ref, who, HEAD_WIDTH),
            own_rows(vbuf),
            sent_sem.at[1],
            value_sem.at[me],
        )
        asked = [query_part(who, chunk) for chunk in range(chunks)]
        return [key_block, asked[0], value_block] + asked[1:]

    for source, target, _, landed in blocks_for(me):
        pltpu.make_async_copy(source, target, landed).start()

    order = [(0, 1, 1), (1, 1, 1), (0, 1, 0), (0, 0, 1), (1, 1, 0), (1, 0, 1), (1, 0, 0)]
    barrier = pltpu.get_barrier_semaphore()
    for flip in order:
        pl.semaphore_signal(barrier, inc=1, device_id=(section, peer(*flip)), device_id_type=MESH)

    @pl.when(section > 0)
    def _():
        pl.semaphore_signal(barrier, inc=1, device_id=(section - 1, me), device_id_type=MESH)

    @pl.when(section < sections - 1)
    def _():
        pl.semaphore_signal(barrier, inc=1, device_id=(section + 1, me), device_id_type=MESH)

    pl.semaphore_wait(barrier, len(order) + has_prev + has_next)

    def exchange(who):
        return [
            pltpu.make_async_remote_copy(
                src_ref=source,
                dst_ref=target,
                send_sem=sent,
                recv_sem=landed,
                device_id=(section, who),
                device_id_type=MESH,
            )
            for source, target, sent, landed in blocks_for(who)
        ]

    for wave in zip(*[exchange(peer(*flip)) for flip in order]):
        for copy in wave:
            copy.start()

    def arrive(target, sem):
        pltpu.make_async_copy(target, target, sem).wait()

    narrow = jnp.bfloat16
    factor = QUERY_SCALAR ** (-0.5) * math.log2(math.e)
    group = query_width // HEAD_WIDTH
    asks = devices * group * chunk_rows
    low_asks, low_keys = asks // 2, devices * rows // 2

    def column_positions(chunk):
        lane = lax.broadcasted_iota(jnp.int32, (1, asks), 1)
        block = lane // (group * chunk_rows)
        return block * rows + chunk * chunk_rows + lane % chunk_rows

    def visible(scores, first_key, positions):
        key = lax.broadcasted_iota(jnp.int32, scores.shape, 0) + first_key
        return jnp.where(key <= positions, scores, -jnp.inf)

    def score(key_rows, query_rows):
        return lax.dot_general(
            key_rows, query_rows, (((1,), (1,)), ((), ())), preferred_element_type=jnp.float32
        )

    def turn_values():
        for block in range(devices):
            span = pl.ds(block * rows, rows)
            arrive(vbuf.at[span], value_sem.at[block])
            vturned[:, block * rows : (block + 1) * rows] = vbuf[span].T

    def weigh(chunk):
        arrive(qbuf.at[chunk], query_sem.at[chunk])
        asked = jnp.concatenate(
            [
                qbuf[chunk, block, :, head * HEAD_WIDTH : (head + 1) * HEAD_WIDTH]
                for block in range(devices)
                for head in range(group)
            ],
            axis=0,
        )
        positions = column_positions(chunk)
        early = score(kbuf[:low_keys], asked)
        late = score(kbuf[low_keys:], asked[low_asks:])
        left = visible(early[:, :low_asks], 0, positions[:, :low_asks])
        right = early[:, low_asks:]
        late = visible(late, low_keys, positions[:, low_asks:])
        left_top = jnp.max(left, axis=0, keepdims=True)
        right_top = jnp.maximum(
            jnp.max(right, axis=0, keepdims=True), jnp.max(late, axis=0, keepdims=True)
        )
        left = jnp.exp2((left - left_top) * factor)
        right = jnp.exp2((right - right_top) * factor)
        late = jnp.exp2((late - right_top) * factor)
        left_total = jnp.sum(left, axis=0, keepdims=True)
        right_total = jnp.sum(right, axis=0, keepdims=True) + jnp.sum(late, axis=0, keepdims=True)
        early = jnp.concatenate([left.astype(narrow), right.astype(narrow)], axis=1)
        return early, late.astype(narrow), left_total, right_total

    def mix(chunk, early, late, left_total, right_total):
        mixed = jnp.dot(vturned[:, :low_keys], early, preferred_element_type=jnp.float32)
        mixed_late = jnp.dot(vturned[:, low_keys:], late, preferred_element_type=jnp.float32)
        halves = (
            mixed[:, :low_asks] / left_total,
            (mixed[:, low_asks:] + mixed_late) / right_total,
        )
        for index, part in enumerate(halves):
            turned = part.T.astype(narrow)
            for within in range(devices // 2):
                block = index * (devices // 2) + within
                for head in range(group):
                    start = (within * group + head) * chunk_rows
                    att[
                        block % 2,
                        chunk,
                        block // 2,
                        :,
                        head * HEAD_WIDTH : (head + 1) * HEAD_WIDTH,
                    ] = turned[start : start + chunk_rows]

    def remote(source, target, sent, landed, who):
        return pltpu.make_async_remote_copy(
            src_ref=source,
            dst_ref=target,
            send_sem=sent,
            recv_sem=landed,
            device_id=who,
            device_id_type=MESH,
        )

    def pair_copy(piece):
        return remote(
            pair_out.at[piece],
            pair_in.at[piece],
            sent_sem.at[3],
            pair_sem.at[piece],
            (section, sibling),
        )

    low, high = pl.ds(0, half), pl.ds(half, width - half)

    def x1_copy(piece):
        target = first_in.at[piece, :, :, low]
        return remote(
            x1_out.at[piece], target, sent_sem.at[4], first_sem.at[piece], (section, beside)
        )

    def y1_copy(piece):
        target = first_in.at[piece, :, :, high]
        return remote(
            y1_out.at[piece], target, sent_sem.at[5], first_sem.at[piece], (section, above)
        )

    def x2_copy(piece):
        target = second_in.at[piece, :, high]
        return remote(
            x2_out.at[piece], target, sent_sem.at[6], second_sem.at[piece], (section, beside)
        )

    def y2_copy(piece):
        target = second_in.at[piece, :, low]
        return remote(
            y2_out.at[piece], target, sent_sem.at[7], second_sem.at[piece], (section, above)
        )

    def chain_copy(piece):
        onward = (jnp.minimum(section + 1, sections - 1), me)
        return remote(
            out_ref.at[piece], base.at[piece], sent_sem.at[8], chain_sem.at[piece], onward
        )

    chip_count = pair_count
    places = [who // 2 for who in (beside, diagonal, above, me)]

    def product(chunk):
        theirs = chip_count * chunk_rows
        left = jnp.concatenate(
            [att[1 - core, chunk].reshape(theirs, query_width)]
            + [att[core, chunk, place] for place in places],
            axis=0,
        )
        for at, span in column_tiles(0, width, TILE):
            part = jnp.dot(left, w_ref[:, at : at + span], preferred_element_type=jnp.float32)
            part = part.reshape(2, chip_count, pieces, piece_rows, span)
            for index in range(pieces):
                piece = chunk * pieces + index
                pair_out[piece, :, :, at : at + span] = part[0, :, index].astype(narrow)
                own[piece, :, :, at : at + span] = part[1, :, index]
        for index in range(pieces):
            pair_copy(chunk * pieces + index).start()

    def first_turn(piece):
        arrive(pair_in.at[piece], pair_sem.at[piece])

        def summed(index, at, stop):
            return own[piece, index, :, at:stop] + pair_in[piece, places[index], :, at:stop].astype(
                jnp.float32
            )

        x1_out[piece, 0] = summed(0, 0, half).astype(narrow)
        x1_out[piece, 1] = summed(1, 0, half).astype(narrow)
        x1_copy(piece).start()
        y1_out[piece, 0] = summed(2, half, width).astype(narrow)
        y1_out[piece, 1] = summed(1, half, width).astype(narrow)
        y1_copy(piece).start()
        keep_y[piece] = summed(2, 0, half)
        keep_x[piece] = summed(0, half, width)
        keep_me[piece] = summed(3, 0, width)

    def second_turn(piece):
        arrive(first_in.at[piece], first_sem.at[piece])
        passing = first_in[piece, 1].astype(jnp.float32)
        y2_out[piece] = (keep_y[piece] + passing[:, :half]).astype(narrow)
        y2_copy(piece).start()
        x2_out[piece] = (keep_x[piece] + passing[:, half:]).astype(narrow)
        x2_copy(piece).start()
        keep_me[piece] += first_in[piece, 0].astype(jnp.float32)

    def normalise(piece):
        arrive(second_in.at[piece], second_sem.at[piece])
        full = keep_me[piece] + second_in[piece].astype(jnp.float32)
        squares = jnp.sum(full * full, axis=1, keepdims=True)
        ratio = lax.rsqrt(squares * (1.0 / width) + norm_eps)
        keep_me[piece] = full * ratio * gains_ref[...].astype(jnp.float32)

    def hand_on(piece):
        arrive(base.at[piece], chain_sem.at[piece])
        out_ref[piece] = (base[piece].astype(jnp.float32) + keep_me[piece]).astype(out_ref.dtype)

        @pl.when(section < sections - 1)
        def _():
            chain_copy(piece).start()

    arrive(kbuf, key_sem)
    weights = weigh(0)
    turn_values()
    mix(0, *weights)
    w_copy.wait()
    gains_copy.wait()

    def turn(step, carry):
        chunk = step // pieces
        fresh = step % pieces == 0

        @pl.when(fresh & (chunk > 0) & (chunk < chunks))
        def _():
            mix(chunk, *weigh(chunk))

        @pl.when(fresh & (chunk < chunks))
        def _():
            product(chunk)

        for lag, stage in (
            (FIRST, first_turn),
            (SECOND, second_turn),
            (LAST, normalise),
            (LAST + HOP * section, hand_on),
        ):
            piece = step - lag

            @pl.when((piece >= 0) & (piece < chunks * pieces))
            def _():
                stage(piece)

        return carry

    lax.fori_loop(0, chunks * pieces + LAST + HOP * (sections - 1), turn, 0)

    sent = (
        kbuf.at[pl.ds(0, (devices - 1) * rows)],
        vbuf.at[pl.ds(0, (devices - 1) * rows)],
        qbuf.at[:, pl.ds(0, devices - 1)],
        pair_out,
        x1_out,
        y1_out,
        x2_out,
        y2_out,
    )
    for index, source in enumerate(sent):
        arrive(source, sent_sem.at[index])

    @pl.when(section < sections - 1)
    def _():
        arrive(out_ref, sent_sem.at[len(sent)])


def settle(held_ref, out_ref, sem):
    copy = pltpu.make_async_copy(held_ref, out_ref, sem)
    copy.start()
    copy.wait()


def by_head(sections, chunks, pieces, stream, queries, keys, values, out_weight, gains):
    devices = lax.axis_size("ctx")
    rows, width = stream.shape
    query_width = queries.shape[2] // devices
    chunk_rows = rows // chunks
    piece_rows, count = chunk_rows // pieces, chunks * pieces
    half = (width // LANES + 1) // 2 * LANES
    other = width - half
    chips = devices // 2
    narrow, wide = jnp.bfloat16, jnp.float32
    anywhere = pl.BlockSpec(memory_space=pltpu.HBM)
    in_vmem = pl.BlockSpec(memory_space=pltpu.VMEM)
    dma = pltpu.SemaphoreType.DMA
    out = pl.pallas_call(
        functools.partial(fused_kernel, sections, chunks, pieces, half),
        out_shape=pltpu.VMEM((count, piece_rows, width), narrow),
        in_specs=[anywhere] * 6,
        out_specs=in_vmem,
        scratch_shapes=[
            pltpu.VMEM((chunks, devices, chunk_rows, query_width), narrow),
            pltpu.VMEM((devices * rows, HEAD_WIDTH), narrow),
            pltpu.VMEM((devices * rows, HEAD_WIDTH), narrow),
            pltpu.VMEM((HEAD_WIDTH, devices * rows), narrow),
            pltpu.VMEM(out_weight.shape[1:], narrow),
            pltpu.VMEM(gains.shape, narrow),
            pltpu.VMEM((2, chunks, chips, chunk_rows, query_width), narrow),
            pltpu.VMEM((count, chips, piece_rows, width), narrow),
            pltpu.VMEM((count, chips, piece_rows, width), narrow),
            pltpu.VMEM((count, 2, piece_rows, half), narrow),
            pltpu.VMEM((count, 2, piece_rows, other), narrow),
            pltpu.VMEM((count, 2, piece_rows, width), narrow),
            pltpu.VMEM((count, piece_rows, other), narrow),
            pltpu.VMEM((count, piece_rows, half), narrow),
            pltpu.VMEM((count, piece_rows, width), narrow),
            pltpu.VMEM((count, chips, piece_rows, width), wide),
            pltpu.VMEM((count, piece_rows, width), wide),
            pltpu.VMEM((count, piece_rows, other), wide),
            pltpu.VMEM((count, piece_rows, half), wide),
            pltpu.VMEM((count, piece_rows, width), narrow),
            dma((2,)),
            dma,
            dma((devices,)),
            dma((chunks,)),
            dma((9,)),
            dma((count,)),
            dma((count,)),
            dma((count,)),
            dma((count,)),
        ],
        compiler_params=pltpu.CompilerParams(
            collective_id=0, has_side_effects=True, vmem_limit_bytes=VMEM_GRANT
        ),
    )(gains, stream, queries[0], keys[0], values[0], out_weight[0])
    return pl.pallas_call(
        settle,
        out_shape=jax.ShapeDtypeStruct(out.shape, out.dtype),
        in_specs=[in_vmem],
        out_specs=anywhere,
        scratch_shapes=[dma(())],
        compiler_params=pltpu.CompilerParams(vmem_limit_bytes=2_000_000),
    )(out).reshape(1, rows, width)


def fits_by_head(mesh, rows):
    devices = mesh.shape["ctx"]
    return devices == KEY_HEADS and devices * rows <= WINDOW_LENGTH and devices % 8 == 0


def solution(mesh):
    in_specs = (
        P("ctx", None),
        P("section", "ctx", None),
        P("section", "ctx", None),
        P("section", "ctx", None),
        P("section", "ctx", None),
        P("section", None),
    )
    out_specs = P("section", "ctx", None)
    sections = mesh.shape["section"]

    def step(stream, *rest):
        rows = stream.shape[0]
        if fits_by_head(mesh, rows):
            return by_head(sections, CHUNKS, PIECES, stream, *rest)
        return local(stream, *rest)

    return jax.shard_map(step, mesh=mesh, in_specs=in_specs, out_specs=out_specs, check_vma=False)
```

```python
import functools
import math

import jax
import jax.numpy as jnp
from jax import lax
from jax.experimental import pallas as pl
from jax.experimental.pallas import tpu as pltpu
from jax.sharding import PartitionSpec as P

KEY_HEADS = 8
HEAD_WIDTH = 128
WINDOW_LENGTH = 1024
QUERY_SCALAR = 168
QUERY_PER_KEY = 2


norm_eps = 1e-06


def passed_along(block, axis, distance):
    devices = range(lax.axis_size(axis))
    route = [(i - distance, i) for i in devices if i - distance in devices]
    return lax.ppermute(block, axis, route)


def attend_block(query_matrix_rows, key_matrix_rows, value_matrix_rows, allowed, scale_factor):
    scores = (
        jnp.einsum(
            "qhgd,khd->hgqk", query_matrix_rows, key_matrix_rows, preferred_element_type=jnp.float32
        )
        * scale_factor
    )
    scores = jnp.where(allowed, scores, -jnp.inf)
    row_top = jnp.max(scores, axis=-1, keepdims=True)
    exponent = jnp.exp(scores - row_top)
    row_total = jnp.sum(exponent, axis=-1, keepdims=True)
    weights = exponent.astype(jnp.bfloat16)
    mixed_rows = jnp.einsum(
        "hgqk,khd->qhgd", weights, value_matrix_rows, preferred_element_type=jnp.float32
    )
    return mixed_rows / jnp.transpose(row_total, (2, 0, 1, 3))


def local(stream, queries, keys, values, out_weight, gains):
    tok_rows = stream.shape[0]
    span_rows = min(tok_rows, WINDOW_LENGTH)
    hop_count = WINDOW_LENGTH // span_rows
    own_tail = (keys[0, tok_rows - span_rows :], values[0, tok_rows - span_rows :])
    pieces = [
        passed_along((own_tail[0], own_tail[1]), "ctx", distance)
        for distance in range(hop_count, 0, -1)
    ]
    key_matrix_rows = jnp.concatenate([piece_pair[0] for piece_pair in pieces] + [keys[0]], axis=0)
    value_matrix_rows = jnp.concatenate(
        [piece_pair[1] for piece_pair in pieces] + [values[0]], axis=0
    )
    ctx_base = lax.axis_index("ctx") * tok_rows
    query_pos = ctx_base + jnp.arange(tok_rows, dtype=jnp.int32)
    key_pos = ctx_base - WINDOW_LENGTH + jnp.arange(WINDOW_LENGTH + tok_rows, dtype=jnp.int32)
    allowed = (
        (key_pos[None, :] >= 0)
        & (key_pos[None, :] <= query_pos[:, None])
        & (key_pos[None, :] > query_pos[:, None] - WINDOW_LENGTH)
    )
    scale_factor = QUERY_SCALAR ** (-0.5)
    heads_per_block = math.gcd(KEY_HEADS, 4)
    query_width = heads_per_block * QUERY_PER_KEY * HEAD_WIDTH
    key_width = heads_per_block * HEAD_WIDTH
    outputs_list = []
    for query_head_group in range(KEY_HEADS // heads_per_block):
        query_cols = queries[
            0, :, query_head_group * query_width : (query_head_group + 1) * query_width
        ].reshape(tok_rows, heads_per_block, QUERY_PER_KEY, HEAD_WIDTH)
        key_cols = key_matrix_rows[
            :, query_head_group * key_width : (query_head_group + 1) * key_width
        ].reshape(WINDOW_LENGTH + tok_rows, heads_per_block, HEAD_WIDTH)
        value_cols = value_matrix_rows[
            :, query_head_group * key_width : (query_head_group + 1) * key_width
        ].reshape(WINDOW_LENGTH + tok_rows, heads_per_block, HEAD_WIDTH)
        mixed_rows = attend_block(query_cols, key_cols, value_cols, allowed, scale_factor)
        outputs_list.append(mixed_rows.reshape(tok_rows, query_width))
    attended = jnp.concatenate(outputs_list, axis=1).astype(jnp.bfloat16)
    projected = jnp.dot(
        attended,
        lax.all_gather(out_weight[0], "ctx", axis=0, tiled=True),
        preferred_element_type=jnp.float32,
    )
    mean_square = jnp.mean(projected * projected, axis=-1, keepdims=True)
    branch = projected * lax.rsqrt(mean_square + norm_eps) * gains[0].astype(jnp.float32)
    section_index = lax.axis_index("section")
    section_count = lax.axis_size("section")
    running = jnp.where(
        section_index == 0, stream.astype(jnp.float32) + branch, jnp.zeros_like(branch)
    )
    for turn_index in range(section_count - 1):
        arrived = passed_along(running.astype(jnp.bfloat16), "section", 1).astype(running.dtype)
        running = jnp.where(section_index == turn_index + 1, arrived + branch, running)
    return running.astype(jnp.bfloat16)[None]


LANES = 128
MESH = pl.DeviceIdType.MESH
CHUNKS = 8
PIECES = 2
FIRST = 1
SECOND = 4
LAST = 7
HOP = 2
TILE = 512
VMEM_GRANT = 60_000_000


def column_tiles(start, stop, width):
    return [(at, min(at + width, stop) - at) for at in range(start, stop, width)]


def fused_kernel(
    sections,
    chunks,
    pieces,
    half,
    gains_hbm,
    stream_ref,
    q_ref,
    k_ref,
    v_ref,
    w_hbm,
    out_ref,
    qbuf,
    kbuf,
    vbuf,
    vturned,
    w_ref,
    gains_ref,
    att,
    pair_out,
    pair_in,
    far_x,
    far_y,
    first_in,
    near_x,
    near_y,
    onward_x,
    onward_y,
    second_in,
    own,
    keep_me,
    keep_x,
    keep_y,
    base,
    local_sem,
    key_sem,
    value_sem,
    query_sem,
    sent_sem,
    pair_sem,
    first_sem,
    second_sem,
    chain_sem,
):
    me = lax.axis_index("ctx")
    section = lax.axis_index("section")
    devices, chunk_rows, query_width = qbuf.shape[1:]
    width = w_ref.shape[1]
    rows = chunks * chunk_rows
    piece_rows = chunk_rows // pieces
    quarter, pair_count = devices // 4, devices // 2
    core = me % 2
    across = (me // quarter) % 2
    up = me // pair_count
    flips = (1 - 2 * core, quarter * (1 - 2 * across), pair_count * (1 - 2 * up))

    def peer(flip_core, flip_x, flip_y):
        return me + flips[0] * flip_core + flips[1] * flip_x + flips[2] * flip_y

    sibling, beside, above, diagonal = peer(1, 0, 0), peer(0, 1, 0), peer(0, 0, 1), peer(0, 1, 1)
    has_prev = jnp.minimum(section, 1)
    has_next = jnp.minimum(sections - 1 - section, 1)

    def own_rows(buf):
        return buf.at[pl.ds(pl.multiple_of(me * rows, rows), rows)]

    def head_columns(ref, who, span):
        return ref.at[:, pl.ds(pl.multiple_of(who * span, span), span)]

    w_copy = pltpu.make_async_copy(w_hbm, w_ref, local_sem.at[0])
    w_copy.start()
    gains_copy = pltpu.make_async_copy(gains_hbm, gains_ref, local_sem.at[1])
    gains_copy.start()

    @pl.when(section == 0)
    def _():
        for piece in range(chunks * pieces):
            pltpu.make_async_copy(
                stream_ref.at[pl.ds(piece * piece_rows, piece_rows)],
                base.at[piece],
                chain_sem.at[piece],
            ).start()

    def query_part(who, chunk):
        source = q_ref.at[
            pl.ds(chunk * chunk_rows, chunk_rows),
            pl.ds(pl.multiple_of(who * query_width, query_width), query_width),
        ]
        return source, qbuf.at[chunk, me], sent_sem.at[2], query_sem.at[chunk]

    def blocks_for(who):
        key_block = head_columns(k_ref, who, HEAD_WIDTH), own_rows(kbuf), sent_sem.at[0], key_sem
        value_block = (
            head_columns(v_ref, who, HEAD_WIDTH),
            own_rows(vbuf),
            sent_sem.at[1],
            value_sem.at[me // pair_count],
        )
        asked = [query_part(who, chunk) for chunk in range(chunks)]
        return [key_block, asked[0], value_block] + asked[1:]

    for source, target, _, landed in blocks_for(me):
        pltpu.make_async_copy(source, target, landed).start()

    order = [(0, 1, 1), (1, 1, 1), (0, 1, 0), (0, 0, 1), (1, 1, 0), (1, 0, 1), (1, 0, 0)]
    barrier = pltpu.get_barrier_semaphore()
    for flip in order:
        pl.semaphore_signal(barrier, inc=1, device_id=(section, peer(*flip)), device_id_type=MESH)

    @pl.when(section > 0)
    def _():
        pl.semaphore_signal(barrier, inc=1, device_id=(section - 1, me), device_id_type=MESH)

    @pl.when(section < sections - 1)
    def _():
        pl.semaphore_signal(barrier, inc=1, device_id=(section + 1, me), device_id_type=MESH)

    pl.semaphore_wait(barrier, len(order) + has_prev + has_next)

    def exchange(who):
        return [
            pltpu.make_async_remote_copy(
                src_ref=source,
                dst_ref=target,
                send_sem=sent,
                recv_sem=landed,
                device_id=(section, who),
                device_id_type=MESH,
            )
            for source, target, sent, landed in blocks_for(who)
        ]

    for wave in zip(*[exchange(peer(*flip)) for flip in order]):
        for copy in wave:
            copy.start()

    def arrive(target, sem):
        pltpu.make_async_copy(target, target, sem).wait()

    narrow = jnp.bfloat16
    factor = QUERY_SCALAR ** (-0.5) * math.log2(math.e)
    group = query_width // HEAD_WIDTH
    asks = devices * group * chunk_rows
    low_asks, low_keys = asks // 2, devices * rows // 2

    def column_positions(chunk):
        lane = lax.broadcasted_iota(jnp.int32, (1, asks), 1)
        block = lane // (group * chunk_rows)
        return block * rows + chunk * chunk_rows + lane % chunk_rows

    def visible(scores, first_key, positions):
        key = lax.broadcasted_iota(jnp.int32, scores.shape, 0) + first_key
        return jnp.where(key <= positions, scores, -jnp.inf)

    def score(key_rows, query_rows):
        return lax.dot_general(
            key_rows, query_rows, (((1,), (1,)), ((), ())), preferred_element_type=jnp.float32
        )

    def turn_values():
        for side in range(2):
            span = pl.ds(side * low_keys, low_keys)
            arrive(vbuf.at[span], value_sem.at[side])
            vturned[:, side * low_keys : (side + 1) * low_keys] = vbuf[span].T

    def weigh(chunk):
        arrive(qbuf.at[chunk], query_sem.at[chunk])
        asked = jnp.concatenate(
            [
                qbuf[chunk, block, :, head * HEAD_WIDTH : (head + 1) * HEAD_WIDTH]
                for block in range(devices)
                for head in range(group)
            ],
            axis=0,
        )
        positions = column_positions(chunk)
        early = score(kbuf[:low_keys], asked)
        late = score(kbuf[low_keys:], asked[low_asks:])
        left = visible(early[:, :low_asks], 0, positions[:, :low_asks])
        right = early[:, low_asks:]
        late = visible(late, low_keys, positions[:, low_asks:])
        left_top = jnp.max(left, axis=0, keepdims=True)
        right_top = jnp.maximum(
            jnp.max(right, axis=0, keepdims=True), jnp.max(late, axis=0, keepdims=True)
        )
        left = jnp.exp2((left - left_top) * factor)
        right = jnp.exp2((right - right_top) * factor)
        late = jnp.exp2((late - right_top) * factor)
        left_total = jnp.sum(left, axis=0, keepdims=True)
        right_total = jnp.sum(right, axis=0, keepdims=True) + jnp.sum(late, axis=0, keepdims=True)
        early = jnp.concatenate([left.astype(narrow), right.astype(narrow)], axis=1)
        return early, late.astype(narrow), left_total, right_total

    def mix(chunk, early, late, left_total, right_total):
        mixed = jnp.dot(vturned[:, :low_keys], early, preferred_element_type=jnp.float32)
        mixed_late = jnp.dot(vturned[:, low_keys:], late, preferred_element_type=jnp.float32)
        halves = (
            mixed[:, :low_asks] / left_total,
            (mixed[:, low_asks:] + mixed_late) / right_total,
        )
        for index, part in enumerate(halves):
            turned = part.T.astype(narrow)
            for within in range(devices // 2):
                block = index * (devices // 2) + within
                for head in range(group):
                    start = (within * group + head) * chunk_rows
                    att[
                        block % 2,
                        chunk,
                        block // 2,
                        :,
                        head * HEAD_WIDTH : (head + 1) * HEAD_WIDTH,
                    ] = turned[start : start + chunk_rows]

    def remote(source, target, sent, landed, who):
        return pltpu.make_async_remote_copy(
            src_ref=source,
            dst_ref=target,
            send_sem=sent,
            recv_sem=landed,
            device_id=who,
            device_id_type=MESH,
        )

    def pair_copy(chunk):
        span = pl.ds(chunk * pieces, pieces)
        landed = pair_sem.at[chunk % pair_sem.shape[0]]
        return remote(
            pair_out.at[span], pair_in.at[span], sent_sem.at[3], landed, (section, sibling)
        )

    low, high = pl.ds(0, half), pl.ds(half, width - half)

    def first_copies(piece):
        landed = first_sem.at[piece % first_sem.shape[0]]
        for source, columns, who in ((far_x, low, beside), (far_y, high, above)):
            target = first_in.at[piece, :, columns]
            remote(source.at[piece], target, sent_sem.at[4], landed, (section, who)).start()

    def second_copies(piece, which):
        landed = second_sem.at[piece]
        sends = (
            ((near_x, low, beside), (near_y, high, above)),
            ((onward_y, low, above), (onward_x, high, beside)),
        )
        for source, columns, who in sends[which]:
            target = second_in.at[piece, which, :, columns]
            remote(source.at[piece], target, sent_sem.at[5], landed, (section, who)).start()

    def chain_copy(piece):
        onward = (jnp.minimum(section + 1, sections - 1), me)
        return remote(
            out_ref.at[piece], base.at[piece], sent_sem.at[6], chain_sem.at[piece], onward
        )

    chip_count = pair_count
    places = [who // 2 for who in (beside, diagonal, above, me)]

    def product(chunk):
        theirs = chip_count * chunk_rows
        left = jnp.concatenate(
            [att[1 - core, chunk].reshape(theirs, query_width)]
            + [att[core, chunk, place] for place in places],
            axis=0,
        )
        for at, span in column_tiles(0, width, TILE):
            part = jnp.dot(left, w_ref[:, at : at + span], preferred_element_type=jnp.float32)
            part = part.reshape(2, chip_count, pieces, piece_rows, span)
            for index in range(pieces):
                piece = chunk * pieces + index
                pair_out[piece, :, :, at : at + span] = part[0, :, index].astype(narrow)
                own[piece, :, :, at : at + span] = part[1, :, index]
        pair_copy(chunk).start()

    def first_turn(piece):
        chunk = piece // pieces

        @pl.when(piece % pieces == 0)
        def _():
            span = pl.ds(chunk * pieces, pieces)
            arrive(pair_in.at[span], pair_sem.at[chunk % pair_sem.shape[0]])

        def summed(index, at, stop):
            return own[piece, index, :, at:stop] + pair_in[piece, places[index], :, at:stop].astype(
                jnp.float32
            )

        far_x[piece] = summed(1, 0, half).astype(narrow)
        far_y[piece] = summed(1, half, width).astype(narrow)
        first_copies(piece)
        near_x[piece] = summed(0, 0, half).astype(narrow)
        near_y[piece] = summed(2, half, width).astype(narrow)
        second_copies(piece, 0)
        keep_y[piece] = summed(2, 0, half)
        keep_x[piece] = summed(0, half, width)
        keep_me[piece] = summed(3, 0, width)

    def second_turn(piece):
        arrive(first_in.at[piece], first_sem.at[piece % first_sem.shape[0]])
        passing = first_in[piece].astype(jnp.float32)
        onward_y[piece] = (keep_y[piece] + passing[:, :half]).astype(narrow)
        onward_x[piece] = (keep_x[piece] + passing[:, half:]).astype(narrow)
        second_copies(piece, 1)

    def normalise(piece):
        arrive(second_in.at[piece], second_sem.at[piece])
        received = second_in[piece].astype(jnp.float32)
        full = keep_me[piece] + received[0] + received[1]
        squares = jnp.sum(full * full, axis=1, keepdims=True)
        ratio = lax.rsqrt(squares * (1.0 / width) + norm_eps)
        keep_me[piece] = full * ratio * gains_ref[...].astype(jnp.float32)

    def hand_on(piece):
        arrive(base.at[piece], chain_sem.at[piece])
        out_ref[piece] = (base[piece].astype(jnp.float32) + keep_me[piece]).astype(out_ref.dtype)

        @pl.when(section < sections - 1)
        def _():
            chain_copy(piece).start()

    arrive(kbuf, key_sem)
    weights = weigh(0)
    turn_values()
    mix(0, *weights)
    w_copy.wait()
    gains_copy.wait()
    product(0)

    def turn(step, carry):
        def staged(lag, stage):
            piece = step - lag

            @pl.when((piece >= 0) & (piece < chunks * pieces))
            def _():
                stage(piece)

        staged(FIRST, first_turn)
        chunk = step // pieces + 1

        @pl.when((step % pieces == 0) & (chunk < chunks))
        def _():
            mix(chunk, *weigh(chunk))
            product(chunk)

        staged(SECOND, second_turn)
        staged(LAST, normalise)
        staged(LAST + HOP * section, hand_on)
        return carry

    lax.fori_loop(0, chunks * pieces + LAST + HOP * (sections - 1), turn, 0)

    sent = (
        kbuf.at[pl.ds(0, (devices - 1) * rows)],
        vbuf.at[pl.ds(0, (devices - 1) * rows)],
        qbuf.at[:, pl.ds(0, devices - 1)],
        pair_out,
        first_in,
        second_in,
    )
    for index, source in enumerate(sent):
        arrive(source, sent_sem.at[index])

    @pl.when(section < sections - 1)
    def _():
        arrive(out_ref, sent_sem.at[len(sent)])


def settle(held_ref, out_ref, sem):
    copy = pltpu.make_async_copy(held_ref, out_ref, sem)
    copy.start()
    copy.wait()


def by_head(sections, chunks, pieces, stream, queries, keys, values, out_weight, gains):
    devices = lax.axis_size("ctx")
    rows, width = stream.shape
    query_width = queries.shape[2] // devices
    chunk_rows = rows // chunks
    piece_rows, count = chunk_rows // pieces, chunks * pieces
    half = (width // LANES + 1) // 2 * LANES
    other = width - half
    chips = devices // 2
    narrow, wide = jnp.bfloat16, jnp.float32
    anywhere = pl.BlockSpec(memory_space=pltpu.HBM)
    in_vmem = pl.BlockSpec(memory_space=pltpu.VMEM)
    dma = pltpu.SemaphoreType.DMA
    out = pl.pallas_call(
        functools.partial(fused_kernel, sections, chunks, pieces, half),
        out_shape=pltpu.VMEM((count, piece_rows, width), narrow),
        in_specs=[anywhere] * 6,
        out_specs=in_vmem,
        scratch_shapes=[
            pltpu.VMEM((chunks, devices, chunk_rows, query_width), narrow),
            pltpu.VMEM((devices * rows, HEAD_WIDTH), narrow),
            pltpu.VMEM((devices * rows, HEAD_WIDTH), narrow),
            pltpu.VMEM((HEAD_WIDTH, devices * rows), narrow),
            pltpu.VMEM(out_weight.shape[1:], narrow),
            pltpu.VMEM(gains.shape, narrow),
            pltpu.VMEM((2, chunks, chips, chunk_rows, query_width), narrow),
            pltpu.VMEM((count, chips, piece_rows, width), narrow),
            pltpu.VMEM((count, chips, piece_rows, width), narrow),
            pltpu.VMEM((count, piece_rows, half), narrow),
            pltpu.VMEM((count, piece_rows, other), narrow),
            pltpu.VMEM((count, piece_rows, width), narrow),
            pltpu.VMEM((count, piece_rows, half), narrow),
            pltpu.VMEM((count, piece_rows, other), narrow),
            pltpu.VMEM((count, piece_rows, other), narrow),
            pltpu.VMEM((count, piece_rows, half), narrow),
            pltpu.VMEM((count, 2, piece_rows, width), narrow),
            pltpu.VMEM((count, chips, piece_rows, width), wide),
            pltpu.VMEM((count, piece_rows, width), wide),
            pltpu.VMEM((count, piece_rows, other), wide),
            pltpu.VMEM((count, piece_rows, half), wide),
            pltpu.VMEM((count, piece_rows, width), narrow),
            dma((2,)),
            dma,
            dma((2,)),
            dma((chunks,)),
            dma((7,)),
            dma((min(chunks, 4),)),
            dma((min(count, 8),)),
            dma((count,)),
            dma((count,)),
        ],
        compiler_params=pltpu.CompilerParams(
            collective_id=0, has_side_effects=True, vmem_limit_bytes=VMEM_GRANT
        ),
    )(gains, stream, queries[0], keys[0], values[0], out_weight[0])
    return pl.pallas_call(
        settle,
        out_shape=jax.ShapeDtypeStruct(out.shape, out.dtype),
        in_specs=[in_vmem],
        out_specs=anywhere,
        scratch_shapes=[dma(())],
        compiler_params=pltpu.CompilerParams(vmem_limit_bytes=2_000_000),
    )(out).reshape(1, rows, width)


def fits_by_head(mesh, rows):
    devices = mesh.shape["ctx"]
    return devices == KEY_HEADS and devices * rows <= WINDOW_LENGTH and devices % 8 == 0


def solution(mesh):
    in_specs = (
        P("ctx", None),
        P("section", "ctx", None),
        P("section", "ctx", None),
        P("section", "ctx", None),
        P("section", "ctx", None),
        P("section", None),
    )
    out_specs = P("section", "ctx", None)
    sections = mesh.shape["section"]

    def step(stream, *rest):
        rows = stream.shape[0]
        if fits_by_head(mesh, rows):
            return by_head(sections, CHUNKS, PIECES, stream, *rest)
        return local(stream, *rest)

    return jax.shard_map(step, mesh=mesh, in_specs=in_specs, out_specs=out_specs, check_vma=False)
```

```python
import functools
import math

import jax
import jax.numpy as jnp
from jax import lax
from jax.experimental import pallas as pl
from jax.experimental.pallas import tpu as pltpu
from jax.sharding import PartitionSpec as P

KEY_HEADS = 8
HEAD_WIDTH = 128
WINDOW_LENGTH = 1024
QUERY_SCALAR = 168
QUERY_PER_KEY = 2


norm_eps = 1e-06


def passed_along(block, axis, distance):
    devices = range(lax.axis_size(axis))
    route = [(i - distance, i) for i in devices if i - distance in devices]
    return lax.ppermute(block, axis, route)


def attend_block(query_matrix_rows, key_matrix_rows, value_matrix_rows, allowed, scale_factor):
    scores = (
        jnp.einsum(
            "qhgd,khd->hgqk", query_matrix_rows, key_matrix_rows, preferred_element_type=jnp.float32
        )
        * scale_factor
    )
    scores = jnp.where(allowed, scores, -jnp.inf)
    row_top = jnp.max(scores, axis=-1, keepdims=True)
    exponent = jnp.exp(scores - row_top)
    row_total = jnp.sum(exponent, axis=-1, keepdims=True)
    weights = exponent.astype(jnp.bfloat16)
    mixed_rows = jnp.einsum(
        "hgqk,khd->qhgd", weights, value_matrix_rows, preferred_element_type=jnp.float32
    )
    return mixed_rows / jnp.transpose(row_total, (2, 0, 1, 3))


def local(stream, queries, keys, values, out_weight, gains):
    tok_rows = stream.shape[0]
    span_rows = min(tok_rows, WINDOW_LENGTH)
    hop_count = WINDOW_LENGTH // span_rows
    own_tail = (keys[0, tok_rows - span_rows :], values[0, tok_rows - span_rows :])
    pieces = [
        passed_along((own_tail[0], own_tail[1]), "ctx", distance)
        for distance in range(hop_count, 0, -1)
    ]
    key_matrix_rows = jnp.concatenate([piece_pair[0] for piece_pair in pieces] + [keys[0]], axis=0)
    value_matrix_rows = jnp.concatenate(
        [piece_pair[1] for piece_pair in pieces] + [values[0]], axis=0
    )
    ctx_base = lax.axis_index("ctx") * tok_rows
    query_pos = ctx_base + jnp.arange(tok_rows, dtype=jnp.int32)
    key_pos = ctx_base - WINDOW_LENGTH + jnp.arange(WINDOW_LENGTH + tok_rows, dtype=jnp.int32)
    allowed = (
        (key_pos[None, :] >= 0)
        & (key_pos[None, :] <= query_pos[:, None])
        & (key_pos[None, :] > query_pos[:, None] - WINDOW_LENGTH)
    )
    scale_factor = QUERY_SCALAR ** (-0.5)
    heads_per_block = math.gcd(KEY_HEADS, 4)
    query_width = heads_per_block * QUERY_PER_KEY * HEAD_WIDTH
    key_width = heads_per_block * HEAD_WIDTH
    outputs_list = []
    for query_head_group in range(KEY_HEADS // heads_per_block):
        query_cols = queries[
            0, :, query_head_group * query_width : (query_head_group + 1) * query_width
        ].reshape(tok_rows, heads_per_block, QUERY_PER_KEY, HEAD_WIDTH)
        key_cols = key_matrix_rows[
            :, query_head_group * key_width : (query_head_group + 1) * key_width
        ].reshape(WINDOW_LENGTH + tok_rows, heads_per_block, HEAD_WIDTH)
        value_cols = value_matrix_rows[
            :, query_head_group * key_width : (query_head_group + 1) * key_width
        ].reshape(WINDOW_LENGTH + tok_rows, heads_per_block, HEAD_WIDTH)
        mixed_rows = attend_block(query_cols, key_cols, value_cols, allowed, scale_factor)
        outputs_list.append(mixed_rows.reshape(tok_rows, query_width))
    attended = jnp.concatenate(outputs_list, axis=1).astype(jnp.bfloat16)
    projected = jnp.dot(
        attended,
        lax.all_gather(out_weight[0], "ctx", axis=0, tiled=True),
        preferred_element_type=jnp.float32,
    )
    mean_square = jnp.mean(projected * projected, axis=-1, keepdims=True)
    branch = projected * lax.rsqrt(mean_square + norm_eps) * gains[0].astype(jnp.float32)
    section_index = lax.axis_index("section")
    section_count = lax.axis_size("section")
    running = jnp.where(
        section_index == 0, stream.astype(jnp.float32) + branch, jnp.zeros_like(branch)
    )
    for turn_index in range(section_count - 1):
        arrived = passed_along(running.astype(jnp.bfloat16), "section", 1).astype(running.dtype)
        running = jnp.where(section_index == turn_index + 1, arrived + branch, running)
    return running.astype(jnp.bfloat16)[None]


LANES = 128
MESH = pl.DeviceIdType.MESH
CHUNKS = 8
PIECES = 2
FIRST = 1
SECOND = 4
LAST = 7
HOP = 2
TAIL = 4
TILE = 512
VMEM_GRANT = 60_000_000


def column_tiles(start, stop, width):
    return [(at, min(at + width, stop) - at) for at in range(start, stop, width)]


def fused_kernel(
    sections,
    chunks,
    pieces,
    half,
    gains_hbm,
    stream_ref,
    q_ref,
    k_ref,
    v_ref,
    w_hbm,
    out_ref,
    qbuf,
    kbuf,
    vbuf,
    vturned,
    w_ref,
    gains_ref,
    att,
    pair_out,
    pair_in,
    far,
    first_in,
    near,
    onward,
    second_in,
    own,
    keep_me,
    keep,
    base,
    local_sem,
    key_sem,
    value_sem,
    query_sem,
    sent_sem,
    pair_sem,
    first_sem,
    second_sem,
    chain_sem,
):
    me = lax.axis_index("ctx")
    section = lax.axis_index("section")
    devices, chunk_rows, query_width = qbuf.shape[1:]
    width = w_ref.shape[1]
    rows = chunks * chunk_rows
    piece_rows = chunk_rows // pieces
    quarter, pair_count = devices // 4, devices // 2
    core = me % 2
    across = (me // quarter) % 2
    up = me // pair_count
    flips = (1 - 2 * core, quarter * (1 - 2 * across), pair_count * (1 - 2 * up))

    def peer(flip_core, flip_x, flip_y):
        return me + flips[0] * flip_core + flips[1] * flip_x + flips[2] * flip_y

    sibling, beside, above, diagonal = peer(1, 0, 0), peer(0, 1, 0), peer(0, 0, 1), peer(0, 1, 1)
    has_prev = jnp.minimum(section, 1)
    has_next = jnp.minimum(sections - 1 - section, 1)

    def own_rows(buf):
        return buf.at[pl.ds(pl.multiple_of(me * rows, rows), rows)]

    def head_columns(ref, who, span):
        return ref.at[:, pl.ds(pl.multiple_of(who * span, span), span)]

    tail_start = chunks * pieces - TAIL
    sides = ((0, half), (half, width))

    def hand_parts(late, piece):
        if late:
            return (sides[0], piece), (sides[1], piece + TAIL)
        return (((0, width), piece),)

    w_copy = pltpu.make_async_copy(w_hbm, w_ref, local_sem.at[0])
    w_copy.start()
    gains_copy = pltpu.make_async_copy(gains_hbm, gains_ref, local_sem.at[1])
    gains_copy.start()

    @pl.when(section == 0)
    def _():
        for piece in range(chunks * pieces):
            for (at, stop), landed in hand_parts(piece >= tail_start, piece):
                columns = pl.ds(at, stop - at)
                pltpu.make_async_copy(
                    stream_ref.at[pl.ds(piece * piece_rows, piece_rows), columns],
                    base.at[piece, :, columns],
                    chain_sem.at[landed],
                ).start()

    def query_part(who, chunk):
        source = q_ref.at[
            pl.ds(chunk * chunk_rows, chunk_rows),
            pl.ds(pl.multiple_of(who * query_width, query_width), query_width),
        ]
        return source, qbuf.at[chunk, me], sent_sem.at[2], query_sem.at[chunk]

    def blocks_for(who):
        key_block = head_columns(k_ref, who, HEAD_WIDTH), own_rows(kbuf), sent_sem.at[0], key_sem
        value_block = (
            head_columns(v_ref, who, HEAD_WIDTH),
            own_rows(vbuf),
            sent_sem.at[1],
            value_sem.at[me // pair_count],
        )
        asked = [query_part(who, chunk) for chunk in range(chunks)]
        return [key_block, asked[0], value_block] + asked[1:]

    for source, target, _, landed in blocks_for(me):
        pltpu.make_async_copy(source, target, landed).start()

    order = [(0, 1, 1), (1, 1, 1), (0, 1, 0), (0, 0, 1), (1, 1, 0), (1, 0, 1), (1, 0, 0)]
    barrier = pltpu.get_barrier_semaphore()
    for flip in order:
        pl.semaphore_signal(barrier, inc=1, device_id=(section, peer(*flip)), device_id_type=MESH)

    @pl.when(section > 0)
    def _():
        pl.semaphore_signal(barrier, inc=1, device_id=(section - 1, me), device_id_type=MESH)

    @pl.when(section < sections - 1)
    def _():
        pl.semaphore_signal(barrier, inc=1, device_id=(section + 1, me), device_id_type=MESH)

    pl.semaphore_wait(barrier, len(order) + has_prev + has_next)

    def exchange(who):
        return [
            pltpu.make_async_remote_copy(
                src_ref=source,
                dst_ref=target,
                send_sem=sent,
                recv_sem=landed,
                device_id=(section, who),
                device_id_type=MESH,
            )
            for source, target, sent, landed in blocks_for(who)
        ]

    for wave in zip(*[exchange(peer(*flip)) for flip in order]):
        for copy in wave:
            copy.start()

    def arrive(target, sem):
        pltpu.make_async_copy(target, target, sem).wait()

    narrow = jnp.bfloat16
    factor = QUERY_SCALAR ** (-0.5) * math.log2(math.e)
    group = query_width // HEAD_WIDTH
    asks = devices * group * chunk_rows
    low_asks, low_keys = asks // 2, devices * rows // 2

    def column_positions(chunk):
        lane = lax.broadcasted_iota(jnp.int32, (1, asks), 1)
        block = lane // (group * chunk_rows)
        return block * rows + chunk * chunk_rows + lane % chunk_rows

    def visible(scores, first_key, positions):
        key = lax.broadcasted_iota(jnp.int32, scores.shape, 0) + first_key
        return jnp.where(key <= positions, scores, -jnp.inf)

    def score(key_rows, query_rows):
        return lax.dot_general(
            key_rows, query_rows, (((1,), (1,)), ((), ())), preferred_element_type=jnp.float32
        )

    def turn_values():
        for side in range(2):
            span = pl.ds(side * low_keys, low_keys)
            arrive(vbuf.at[span], value_sem.at[side])
            vturned[:, side * low_keys : (side + 1) * low_keys] = vbuf[span].T

    def weigh(chunk):
        arrive(qbuf.at[chunk], query_sem.at[chunk])
        asked = jnp.concatenate(
            [
                qbuf[chunk, block, :, head * HEAD_WIDTH : (head + 1) * HEAD_WIDTH]
                for block in range(devices)
                for head in range(group)
            ],
            axis=0,
        )
        positions = column_positions(chunk)
        early = score(kbuf[:low_keys], asked)
        late = score(kbuf[low_keys:], asked[low_asks:])
        left = visible(early[:, :low_asks], 0, positions[:, :low_asks])
        right = early[:, low_asks:]
        late = visible(late, low_keys, positions[:, low_asks:])
        left_top = jnp.max(left, axis=0, keepdims=True)
        right_top = jnp.maximum(
            jnp.max(right, axis=0, keepdims=True), jnp.max(late, axis=0, keepdims=True)
        )
        left = jnp.exp2((left - left_top) * factor)
        right = jnp.exp2((right - right_top) * factor)
        late = jnp.exp2((late - right_top) * factor)
        left_total = jnp.sum(left, axis=0, keepdims=True)
        right_total = jnp.sum(right, axis=0, keepdims=True) + jnp.sum(late, axis=0, keepdims=True)
        early = jnp.concatenate([left.astype(narrow), right.astype(narrow)], axis=1)
        return early, late.astype(narrow), left_total, right_total

    def mix(chunk, early, late, left_total, right_total):
        mixed = jnp.dot(vturned[:, :low_keys], early, preferred_element_type=jnp.float32)
        mixed_late = jnp.dot(vturned[:, low_keys:], late, preferred_element_type=jnp.float32)
        halves = (
            mixed[:, :low_asks] / left_total,
            (mixed[:, low_asks:] + mixed_late) / right_total,
        )
        for index, part in enumerate(halves):
            turned = part.T.astype(narrow)
            for within in range(devices // 2):
                block = index * (devices // 2) + within
                for head in range(group):
                    start = (within * group + head) * chunk_rows
                    att[
                        block % 2,
                        chunk,
                        block // 2,
                        :,
                        head * HEAD_WIDTH : (head + 1) * HEAD_WIDTH,
                    ] = turned[start : start + chunk_rows]

    def remote(source, target, sent, landed, who):
        return pltpu.make_async_remote_copy(
            src_ref=source,
            dst_ref=target,
            send_sem=sent,
            recv_sem=landed,
            device_id=who,
            device_id_type=MESH,
        )

    def pair_copy(chunk):
        span = pl.ds(chunk * pieces, pieces)
        landed = pair_sem.at[chunk % pair_sem.shape[0]]
        return remote(
            pair_out.at[span], pair_in.at[span], sent_sem.at[3], landed, (section, sibling)
        )

    def for_each_way(piece, send):
        for odd in range(2):

            @pl.when(piece % 2 == odd)
            def _():
                send(sides[odd], sides[1 - odd])

    def first_copies(piece):
        landed = first_sem.at[piece % first_sem.shape[0]]

        def send(by_x, by_y):
            for (at, stop), who in ((by_x, beside), (by_y, above)):
                part = piece, slice(None), pl.ds(at, stop - at)
                remote(
                    far.at[part], first_in.at[part], sent_sem.at[4], landed, (section, who)
                ).start()

        for_each_way(piece, send)

    def second_copies(piece, which, by_x, by_y):
        for (at, stop), who in ((by_x, beside), (by_y, above)):
            columns = pl.ds(at, stop - at)
            remote(
                (near, onward)[which].at[piece, :, columns],
                second_in.at[piece, which, :, columns],
                sent_sem.at[5],
                second_sem.at[piece],
                (section, who),
            ).start()

    chip_count = pair_count
    places = [who // 2 for who in (beside, diagonal, above, me)]

    def product(chunk):
        theirs = chip_count * chunk_rows
        left = jnp.concatenate(
            [att[1 - core, chunk].reshape(theirs, query_width)]
            + [att[core, chunk, place] for place in places],
            axis=0,
        )
        for at, span in column_tiles(0, width, TILE):
            part = jnp.dot(left, w_ref[:, at : at + span], preferred_element_type=jnp.float32)
            part = part.reshape(2, chip_count, pieces, piece_rows, span)
            for index in range(pieces):
                piece = chunk * pieces + index
                pair_out[piece, :, :, at : at + span] = part[0, :, index].astype(narrow)
                own[piece, :, :, at : at + span] = part[1, :, index]
        pair_copy(chunk).start()

    def first_turn(piece):
        chunk = piece // pieces

        @pl.when(piece % pieces == 0)
        def _():
            span = pl.ds(chunk * pieces, pieces)
            arrive(pair_in.at[span], pair_sem.at[chunk % pair_sem.shape[0]])

        def summed(index, at, stop):
            return own[piece, index, :, at:stop] + pair_in[piece, places[index], :, at:stop].astype(
                jnp.float32
            )

        far[piece] = summed(1, 0, width).astype(narrow)
        first_copies(piece)

        def send(by_x, by_y):
            near[piece, :, by_x[0] : by_x[1]] = summed(0, *by_x).astype(narrow)
            near[piece, :, by_y[0] : by_y[1]] = summed(2, *by_y).astype(narrow)
            second_copies(piece, 0, by_x, by_y)
            keep[piece, :, by_x[0] : by_x[1]] = summed(2, *by_x)
            keep[piece, :, by_y[0] : by_y[1]] = summed(0, *by_y)

        for_each_way(piece, send)
        keep_me[piece] = summed(3, 0, width)

    def second_turn(piece):
        arrive(first_in.at[piece], first_sem.at[piece % first_sem.shape[0]])
        onward[piece] = (keep[piece] + first_in[piece].astype(jnp.float32)).astype(narrow)
        for_each_way(piece, lambda by_x, by_y: second_copies(piece, 1, by_y, by_x))

    def normalise(piece):
        arrive(second_in.at[piece], second_sem.at[piece])
        received = second_in[piece].astype(jnp.float32)
        full = keep_me[piece] + received[0] + received[1]
        squares = jnp.sum(full * full, axis=1, keepdims=True)
        ratio = lax.rsqrt(squares * (1.0 / width) + norm_eps)
        keep_me[piece] = full * ratio * gains_ref[...].astype(jnp.float32)

    onward_device = (jnp.minimum(section + 1, sections - 1), me)

    def hand_parts_on(late, piece):
        for (at, stop), landed in hand_parts(late, piece):
            part = piece, slice(None), pl.ds(at, stop - at)
            arrive(base.at[part], chain_sem.at[landed])
            added = base[piece, :, at:stop].astype(jnp.float32) + keep_me[piece, :, at:stop]
            out_ref[piece, :, at:stop] = added.astype(out_ref.dtype)

            @pl.when(section < sections - 1)
            def _():
                remote(
                    out_ref.at[part],
                    base.at[part],
                    sent_sem.at[6],
                    chain_sem.at[landed],
                    onward_device,
                ).start()

    def hand_on(piece):
        @pl.when(piece < tail_start)
        def _():
            hand_parts_on(False, piece)

        @pl.when(piece >= tail_start)
        def _():
            hand_parts_on(True, piece)

    arrive(kbuf, key_sem)
    weights = weigh(0)
    turn_values()
    mix(0, *weights)
    w_copy.wait()
    gains_copy.wait()
    product(0)

    def turn(step, carry):
        def staged(lag, stage):
            piece = step - lag

            @pl.when((piece >= 0) & (piece < chunks * pieces))
            def _():
                stage(piece)

        staged(FIRST, first_turn)
        chunk = step // pieces + 1

        @pl.when((step % pieces == 0) & (chunk < chunks))
        def _():
            mix(chunk, *weigh(chunk))
            product(chunk)

        staged(SECOND, second_turn)
        staged(LAST, normalise)
        staged(LAST + HOP * section, hand_on)
        return carry

    lax.fori_loop(0, chunks * pieces + LAST + HOP * (sections - 1), turn, 0)

    sent = (
        kbuf.at[pl.ds(0, (devices - 1) * rows)],
        vbuf.at[pl.ds(0, (devices - 1) * rows)],
        qbuf.at[:, pl.ds(0, devices - 1)],
        pair_out,
        first_in,
        second_in,
    )
    for index, source in enumerate(sent):
        arrive(source, sent_sem.at[index])

    @pl.when(section < sections - 1)
    def _():
        arrive(out_ref, sent_sem.at[len(sent)])


def settle(held_ref, out_ref, sem):
    copy = pltpu.make_async_copy(held_ref, out_ref, sem)
    copy.start()
    copy.wait()


def by_head(sections, chunks, pieces, stream, queries, keys, values, out_weight, gains):
    devices = lax.axis_size("ctx")
    rows, width = stream.shape
    query_width = queries.shape[2] // devices
    chunk_rows = rows // chunks
    piece_rows, count = chunk_rows // pieces, chunks * pieces
    half = (width // LANES + 1) // 2 * LANES
    chips = devices // 2
    narrow, wide = jnp.bfloat16, jnp.float32
    anywhere = pl.BlockSpec(memory_space=pltpu.HBM)
    in_vmem = pl.BlockSpec(memory_space=pltpu.VMEM)
    dma = pltpu.SemaphoreType.DMA
    out = pl.pallas_call(
        functools.partial(fused_kernel, sections, chunks, pieces, half),
        out_shape=pltpu.VMEM((count, piece_rows, width), narrow),
        in_specs=[anywhere] * 6,
        out_specs=in_vmem,
        scratch_shapes=[
            pltpu.VMEM((chunks, devices, chunk_rows, query_width), narrow),
            pltpu.VMEM((devices * rows, HEAD_WIDTH), narrow),
            pltpu.VMEM((devices * rows, HEAD_WIDTH), narrow),
            pltpu.VMEM((HEAD_WIDTH, devices * rows), narrow),
            pltpu.VMEM(out_weight.shape[1:], narrow),
            pltpu.VMEM(gains.shape, narrow),
            pltpu.VMEM((2, chunks, chips, chunk_rows, query_width), narrow),
            pltpu.VMEM((count, chips, piece_rows, width), narrow),
            pltpu.VMEM((count, chips, piece_rows, width), narrow),
            pltpu.VMEM((count, piece_rows, width), narrow),
            pltpu.VMEM((count, piece_rows, width), narrow),
            pltpu.VMEM((count, piece_rows, width), narrow),
            pltpu.VMEM((count, piece_rows, width), narrow),
            pltpu.VMEM((count, 2, piece_rows, width), narrow),
            pltpu.VMEM((count, chips, piece_rows, width), wide),
            pltpu.VMEM((count, piece_rows, width), wide),
            pltpu.VMEM((count, piece_rows, width), wide),
            pltpu.VMEM((count, piece_rows, width), narrow),
            dma((2,)),
            dma,
            dma((2,)),
            dma((chunks,)),
            dma((7,)),
            dma((min(chunks, 4),)),
            dma((min(count, 8),)),
            dma((count,)),
            dma((count + TAIL,)),
        ],
        compiler_params=pltpu.CompilerParams(
            collective_id=0, has_side_effects=True, vmem_limit_bytes=VMEM_GRANT
        ),
    )(gains, stream, queries[0], keys[0], values[0], out_weight[0])
    return pl.pallas_call(
        settle,
        out_shape=jax.ShapeDtypeStruct(out.shape, out.dtype),
        in_specs=[in_vmem],
        out_specs=anywhere,
        scratch_shapes=[dma(())],
        compiler_params=pltpu.CompilerParams(vmem_limit_bytes=2_000_000),
    )(out).reshape(1, rows, width)


def fits_by_head(mesh, rows):
    devices = mesh.shape["ctx"]
    return devices == KEY_HEADS and devices * rows <= WINDOW_LENGTH and devices % 8 == 0


def solution(mesh):
    in_specs = (
        P("ctx", None),
        P("section", "ctx", None),
        P("section", "ctx", None),
        P("section", "ctx", None),
        P("section", "ctx", None),
        P("section", None),
    )
    out_specs = P("section", "ctx", None)
    sections = mesh.shape["section"]

    def step(stream, *rest):
        rows = stream.shape[0]
        if fits_by_head(mesh, rows):
            return by_head(sections, CHUNKS, PIECES, stream, *rest)
        return local(stream, *rest)

    return jax.shard_map(step, mesh=mesh, in_specs=in_specs, out_specs=out_specs, check_vma=False)
```

```python
import functools
import math

import jax
import jax.numpy as jnp
from jax import lax
from jax.experimental import pallas as pl
from jax.experimental.pallas import tpu as pltpu
from jax.sharding import PartitionSpec as P

KEY_HEADS = 8
HEAD_WIDTH = 128
WINDOW_LENGTH = 1024
QUERY_SCALAR = 168
QUERY_PER_KEY = 2


norm_eps = 1e-06


def passed_along(block, axis, distance):
    devices = range(lax.axis_size(axis))
    route = [(i - distance, i) for i in devices if i - distance in devices]
    return lax.ppermute(block, axis, route)


def attend_block(query_matrix_rows, key_matrix_rows, value_matrix_rows, allowed, scale_factor):
    scores = (
        jnp.einsum(
            "qhgd,khd->hgqk", query_matrix_rows, key_matrix_rows, preferred_element_type=jnp.float32
        )
        * scale_factor
    )
    scores = jnp.where(allowed, scores, -jnp.inf)
    row_top = jnp.max(scores, axis=-1, keepdims=True)
    exponent = jnp.exp(scores - row_top)
    row_total = jnp.sum(exponent, axis=-1, keepdims=True)
    weights = exponent.astype(jnp.bfloat16)
    mixed_rows = jnp.einsum(
        "hgqk,khd->qhgd", weights, value_matrix_rows, preferred_element_type=jnp.float32
    )
    return mixed_rows / jnp.transpose(row_total, (2, 0, 1, 3))


def local(stream, queries, keys, values, out_weight, gains):
    tok_rows = stream.shape[0]
    span_rows = min(tok_rows, WINDOW_LENGTH)
    hop_count = WINDOW_LENGTH // span_rows
    own_tail = (keys[0, tok_rows - span_rows :], values[0, tok_rows - span_rows :])
    pieces = [
        passed_along((own_tail[0], own_tail[1]), "ctx", distance)
        for distance in range(hop_count, 0, -1)
    ]
    key_matrix_rows = jnp.concatenate([piece_pair[0] for piece_pair in pieces] + [keys[0]], axis=0)
    value_matrix_rows = jnp.concatenate(
        [piece_pair[1] for piece_pair in pieces] + [values[0]], axis=0
    )
    ctx_base = lax.axis_index("ctx") * tok_rows
    query_pos = ctx_base + jnp.arange(tok_rows, dtype=jnp.int32)
    key_pos = ctx_base - WINDOW_LENGTH + jnp.arange(WINDOW_LENGTH + tok_rows, dtype=jnp.int32)
    allowed = (
        (key_pos[None, :] >= 0)
        & (key_pos[None, :] <= query_pos[:, None])
        & (key_pos[None, :] > query_pos[:, None] - WINDOW_LENGTH)
    )
    scale_factor = QUERY_SCALAR ** (-0.5)
    heads_per_block = math.gcd(KEY_HEADS, 4)
    query_width = heads_per_block * QUERY_PER_KEY * HEAD_WIDTH
    key_width = heads_per_block * HEAD_WIDTH
    outputs_list = []
    for query_head_group in range(KEY_HEADS // heads_per_block):
        query_cols = queries[
            0, :, query_head_group * query_width : (query_head_group + 1) * query_width
        ].reshape(tok_rows, heads_per_block, QUERY_PER_KEY, HEAD_WIDTH)
        key_cols = key_matrix_rows[
            :, query_head_group * key_width : (query_head_group + 1) * key_width
        ].reshape(WINDOW_LENGTH + tok_rows, heads_per_block, HEAD_WIDTH)
        value_cols = value_matrix_rows[
            :, query_head_group * key_width : (query_head_group + 1) * key_width
        ].reshape(WINDOW_LENGTH + tok_rows, heads_per_block, HEAD_WIDTH)
        mixed_rows = attend_block(query_cols, key_cols, value_cols, allowed, scale_factor)
        outputs_list.append(mixed_rows.reshape(tok_rows, query_width))
    attended = jnp.concatenate(outputs_list, axis=1).astype(jnp.bfloat16)
    projected = jnp.dot(
        attended,
        lax.all_gather(out_weight[0], "ctx", axis=0, tiled=True),
        preferred_element_type=jnp.float32,
    )
    mean_square = jnp.mean(projected * projected, axis=-1, keepdims=True)
    branch = projected * lax.rsqrt(mean_square + norm_eps) * gains[0].astype(jnp.float32)
    section_index = lax.axis_index("section")
    section_count = lax.axis_size("section")
    running = jnp.where(
        section_index == 0, stream.astype(jnp.float32) + branch, jnp.zeros_like(branch)
    )
    for turn_index in range(section_count - 1):
        arrived = passed_along(running.astype(jnp.bfloat16), "section", 1).astype(running.dtype)
        running = jnp.where(section_index == turn_index + 1, arrived + branch, running)
    return running.astype(jnp.bfloat16)[None]


LANES = 128
MESH = pl.DeviceIdType.MESH
CHUNKS = 8
PIECES = 2
FIRST = 1
NEAR = 2
SECOND = 3
LAST = 6
HOP = 2
TAIL = 4
TILE = 512
VMEM_GRANT = 60_000_000


def column_tiles(start, stop, width):
    return [(at, min(at + width, stop) - at) for at in range(start, stop, width)]


def fused_kernel(
    sections,
    chunks,
    pieces,
    half,
    gains_hbm,
    stream_ref,
    q_ref,
    k_ref,
    v_ref,
    w_hbm,
    out_ref,
    qbuf,
    kbuf,
    vbuf,
    vturned,
    w_ref,
    gains_ref,
    att,
    pair_out,
    pair_in,
    far,
    first_in,
    near,
    onward,
    second_in,
    own,
    keep_me,
    keep,
    base,
    local_sem,
    key_sem,
    value_sem,
    query_sem,
    sent_sem,
    pair_sem,
    first_sem,
    second_sem,
    chain_sem,
):
    me = lax.axis_index("ctx")
    section = lax.axis_index("section")
    devices, chunk_rows, query_width = qbuf.shape[1:]
    width = w_ref.shape[1]
    rows = chunks * chunk_rows
    piece_rows = chunk_rows // pieces
    quarter, pair_count = devices // 4, devices // 2
    core = me % 2
    across = (me // quarter) % 2
    up = me // pair_count
    flips = (1 - 2 * core, quarter * (1 - 2 * across), pair_count * (1 - 2 * up))

    def peer(flip_core, flip_x, flip_y):
        return me + flips[0] * flip_core + flips[1] * flip_x + flips[2] * flip_y

    sibling, beside, above, diagonal = peer(1, 0, 0), peer(0, 1, 0), peer(0, 0, 1), peer(0, 1, 1)
    has_prev = jnp.minimum(section, 1)
    has_next = jnp.minimum(sections - 1 - section, 1)

    def own_rows(buf):
        return buf.at[pl.ds(pl.multiple_of(me * rows, rows), rows)]

    def head_columns(ref, who, span):
        return ref.at[:, pl.ds(pl.multiple_of(who * span, span), span)]

    tail_start = chunks * pieces - TAIL
    sides = ((0, half), (half, width))

    def hand_parts(late, piece):
        if late:
            return (sides[0], piece), (sides[1], piece + TAIL)
        return (((0, width), piece),)

    w_copy = pltpu.make_async_copy(w_hbm, w_ref, local_sem.at[0])
    w_copy.start()
    gains_copy = pltpu.make_async_copy(gains_hbm, gains_ref, local_sem.at[1])
    gains_copy.start()

    @pl.when(section == 0)
    def _():
        for piece in range(chunks * pieces):
            for (at, stop), landed in hand_parts(piece >= tail_start, piece):
                columns = pl.ds(at, stop - at)
                pltpu.make_async_copy(
                    stream_ref.at[pl.ds(piece * piece_rows, piece_rows), columns],
                    base.at[piece, :, columns],
                    chain_sem.at[landed],
                ).start()

    def query_part(who, chunk):
        source = q_ref.at[
            pl.ds(chunk * chunk_rows, chunk_rows),
            pl.ds(pl.multiple_of(who * query_width, query_width), query_width),
        ]
        return source, qbuf.at[chunk, me], sent_sem.at[2], query_sem.at[chunk]

    def blocks_for(who):
        key_block = head_columns(k_ref, who, HEAD_WIDTH), own_rows(kbuf), sent_sem.at[0], key_sem
        value_block = (
            head_columns(v_ref, who, HEAD_WIDTH),
            own_rows(vbuf),
            sent_sem.at[1],
            value_sem.at[me // pair_count],
        )
        asked = [query_part(who, chunk) for chunk in range(chunks)]
        return [key_block, asked[0], value_block] + asked[1:]

    for source, target, _, landed in blocks_for(me):
        pltpu.make_async_copy(source, target, landed).start()

    order = [(0, 1, 1), (1, 1, 1), (0, 1, 0), (0, 0, 1), (1, 1, 0), (1, 0, 1), (1, 0, 0)]
    barrier = pltpu.get_barrier_semaphore()
    for flip in order:
        pl.semaphore_signal(barrier, inc=1, device_id=(section, peer(*flip)), device_id_type=MESH)

    @pl.when(section > 0)
    def _():
        pl.semaphore_signal(barrier, inc=1, device_id=(section - 1, me), device_id_type=MESH)

    @pl.when(section < sections - 1)
    def _():
        pl.semaphore_signal(barrier, inc=1, device_id=(section + 1, me), device_id_type=MESH)

    pl.semaphore_wait(barrier, len(order) + has_prev + has_next)

    def exchange(who):
        return [
            pltpu.make_async_remote_copy(
                src_ref=source,
                dst_ref=target,
                send_sem=sent,
                recv_sem=landed,
                device_id=(section, who),
                device_id_type=MESH,
            )
            for source, target, sent, landed in blocks_for(who)
        ]

    for wave in zip(*[exchange(peer(*flip)) for flip in order]):
        for copy in wave:
            copy.start()

    def arrive(target, sem):
        pltpu.make_async_copy(target, target, sem).wait()

    narrow = jnp.bfloat16
    factor = QUERY_SCALAR ** (-0.5) * math.log2(math.e)
    group = query_width // HEAD_WIDTH
    asks = devices * group * chunk_rows
    low_asks, low_keys = asks // 2, devices * rows // 2

    def column_positions(chunk):
        lane = lax.broadcasted_iota(jnp.int32, (1, asks), 1)
        block = lane // (group * chunk_rows)
        return block * rows + chunk * chunk_rows + lane % chunk_rows

    def visible(scores, first_key, positions):
        key = lax.broadcasted_iota(jnp.int32, scores.shape, 0) + first_key
        return jnp.where(key <= positions, scores, -jnp.inf)

    def score(key_rows, query_rows):
        return lax.dot_general(
            key_rows, query_rows, (((1,), (1,)), ((), ())), preferred_element_type=jnp.float32
        )

    def turn_values():
        for side in range(2):
            span = pl.ds(side * low_keys, low_keys)
            arrive(vbuf.at[span], value_sem.at[side])
            vturned[:, side * low_keys : (side + 1) * low_keys] = vbuf[span].T

    def weigh(chunk):
        arrive(qbuf.at[chunk], query_sem.at[chunk])
        asked = jnp.concatenate(
            [
                qbuf[chunk, block, :, head * HEAD_WIDTH : (head + 1) * HEAD_WIDTH]
                for block in range(devices)
                for head in range(group)
            ],
            axis=0,
        )
        positions = column_positions(chunk)
        early = score(kbuf[:low_keys], asked)
        late = score(kbuf[low_keys:], asked[low_asks:])
        left = visible(early[:, :low_asks], 0, positions[:, :low_asks])
        right = early[:, low_asks:]
        late = visible(late, low_keys, positions[:, low_asks:])
        left_top = jnp.max(left, axis=0, keepdims=True)
        right_top = jnp.maximum(
            jnp.max(right, axis=0, keepdims=True), jnp.max(late, axis=0, keepdims=True)
        )
        left = jnp.exp2((left - left_top) * factor)
        right = jnp.exp2((right - right_top) * factor)
        late = jnp.exp2((late - right_top) * factor)
        left_total = jnp.sum(left, axis=0, keepdims=True)
        right_total = jnp.sum(right, axis=0, keepdims=True) + jnp.sum(late, axis=0, keepdims=True)
        early = jnp.concatenate([left.astype(narrow), right.astype(narrow)], axis=1)
        return early, late.astype(narrow), left_total, right_total

    def mix(chunk, early, late, left_total, right_total):
        mixed = jnp.dot(vturned[:, :low_keys], early, preferred_element_type=jnp.float32)
        mixed_late = jnp.dot(vturned[:, low_keys:], late, preferred_element_type=jnp.float32)
        halves = (
            mixed[:, :low_asks] / left_total,
            (mixed[:, low_asks:] + mixed_late) / right_total,
        )
        for index, part in enumerate(halves):
            turned = part.T.astype(narrow)
            for within in range(devices // 2):
                block = index * (devices // 2) + within
                for head in range(group):
                    start = (within * group + head) * chunk_rows
                    att[
                        block % 2,
                        chunk,
                        block // 2,
                        :,
                        head * HEAD_WIDTH : (head + 1) * HEAD_WIDTH,
                    ] = turned[start : start + chunk_rows]

    def remote(source, target, sent, landed, who):
        return pltpu.make_async_remote_copy(
            src_ref=source,
            dst_ref=target,
            send_sem=sent,
            recv_sem=landed,
            device_id=who,
            device_id_type=MESH,
        )

    def pair_copy(chunk):
        span = pl.ds(chunk * pieces, pieces)
        landed = pair_sem.at[chunk % pair_sem.shape[0]]
        return remote(
            pair_out.at[span], pair_in.at[span], sent_sem.at[3], landed, (section, sibling)
        )

    def for_each_way(piece, send):
        for odd in range(2):

            @pl.when(piece % 2 == odd)
            def _():
                send(sides[odd], sides[1 - odd])

    def first_copies(piece):
        landed = first_sem.at[piece % first_sem.shape[0]]

        def send(by_x, by_y):
            for (at, stop), who in ((by_x, beside), (by_y, above)):
                part = piece, slice(None), pl.ds(at, stop - at)
                remote(
                    far.at[part], first_in.at[part], sent_sem.at[4], landed, (section, who)
                ).start()

        for_each_way(piece, send)

    def second_copies(piece, which, by_x, by_y):
        for (at, stop), who in ((by_x, beside), (by_y, above)):
            columns = pl.ds(at, stop - at)
            remote(
                (near, onward)[which].at[piece, :, columns],
                second_in.at[piece, which, :, columns],
                sent_sem.at[5],
                second_sem.at[piece],
                (section, who),
            ).start()

    chip_count = pair_count
    places = [who // 2 for who in (beside, diagonal, above, me)]

    def product(chunk):
        theirs = chip_count * chunk_rows
        left = jnp.concatenate(
            [att[1 - core, chunk].reshape(theirs, query_width)]
            + [att[core, chunk, place] for place in places],
            axis=0,
        )
        for at, span in column_tiles(0, width, TILE):
            part = jnp.dot(left, w_ref[:, at : at + span], preferred_element_type=jnp.float32)
            part = part.reshape(2, chip_count, pieces, piece_rows, span)
            for index in range(pieces):
                piece = chunk * pieces + index
                pair_out[piece, :, :, at : at + span] = part[0, :, index].astype(narrow)
                own[piece, :, :, at : at + span] = part[1, :, index]
        pair_copy(chunk).start()

    def summed(piece, index, at, stop):
        return own[piece, index, :, at:stop] + pair_in[piece, places[index], :, at:stop].astype(
            jnp.float32
        )

    def send_far(piece):
        chunk = piece // pieces

        @pl.when(piece % pieces == 0)
        def _():
            span = pl.ds(chunk * pieces, pieces)
            arrive(pair_in.at[span], pair_sem.at[chunk % pair_sem.shape[0]])

        far[piece] = summed(piece, 1, 0, width).astype(narrow)
        first_copies(piece)

    def send_near(piece):
        def send(by_x, by_y):
            near[piece, :, by_x[0] : by_x[1]] = summed(piece, 0, *by_x).astype(narrow)
            near[piece, :, by_y[0] : by_y[1]] = summed(piece, 2, *by_y).astype(narrow)
            second_copies(piece, 0, by_x, by_y)
            keep[piece, :, by_x[0] : by_x[1]] = summed(piece, 2, *by_x)
            keep[piece, :, by_y[0] : by_y[1]] = summed(piece, 0, *by_y)

        for_each_way(piece, send)
        keep_me[piece] = summed(piece, 3, 0, width)

    def second_turn(piece):
        arrive(first_in.at[piece], first_sem.at[piece % first_sem.shape[0]])
        onward[piece] = (keep[piece] + first_in[piece].astype(jnp.float32)).astype(narrow)
        for_each_way(piece, lambda by_x, by_y: second_copies(piece, 1, by_y, by_x))

    def normalise(piece):
        arrive(second_in.at[piece], second_sem.at[piece])
        received = second_in[piece].astype(jnp.float32)
        full = keep_me[piece] + received[0] + received[1]
        squares = jnp.sum(full * full, axis=1, keepdims=True)
        ratio = lax.rsqrt(squares * (1.0 / width) + norm_eps)
        keep_me[piece] = full * ratio * gains_ref[...].astype(jnp.float32)

    onward_device = (jnp.minimum(section + 1, sections - 1), me)

    def hand_parts_on(late, piece):
        for (at, stop), landed in hand_parts(late, piece):
            part = piece, slice(None), pl.ds(at, stop - at)
            arrive(base.at[part], chain_sem.at[landed])
            added = base[piece, :, at:stop].astype(jnp.float32) + keep_me[piece, :, at:stop]
            out_ref[piece, :, at:stop] = added.astype(out_ref.dtype)

            @pl.when(section < sections - 1)
            def _():
                remote(
                    out_ref.at[part],
                    base.at[part],
                    sent_sem.at[6],
                    chain_sem.at[landed],
                    onward_device,
                ).start()

    def hand_on(piece):
        @pl.when(piece < tail_start)
        def _():
            hand_parts_on(False, piece)

        @pl.when(piece >= tail_start)
        def _():
            hand_parts_on(True, piece)

    arrive(kbuf, key_sem)
    weights = weigh(0)
    turn_values()
    mix(0, *weights)
    w_copy.wait()
    gains_copy.wait()
    product(0)

    count = chunks * pieces

    def turn(step, carry):
        def staged(lag, stage):
            piece = step - lag

            @pl.when((piece >= 0) & (piece < chunks * pieces))
            def _():
                stage(piece)

        ahead = step - FIRST

        @pl.when((ahead % pieces == 0) & (ahead >= 0) & (ahead < count))
        def _():
            for index in range(pieces):
                send_far(ahead + index)

        staged(NEAR, send_near)
        chunk = step // pieces + 1

        @pl.when((step % pieces == 0) & (chunk < chunks))
        def _():
            mix(chunk, *weigh(chunk))
            product(chunk)

        staged(SECOND, second_turn)
        staged(LAST, normalise)
        staged(LAST + HOP * section, hand_on)
        return carry

    lax.fori_loop(0, chunks * pieces + LAST + HOP * (sections - 1), turn, 0)

    sent = (
        kbuf.at[pl.ds(0, (devices - 1) * rows)],
        vbuf.at[pl.ds(0, (devices - 1) * rows)],
        qbuf.at[:, pl.ds(0, devices - 1)],
        pair_out,
        first_in,
        second_in,
    )
    for index, source in enumerate(sent):
        arrive(source, sent_sem.at[index])

    @pl.when(section < sections - 1)
    def _():
        arrive(out_ref, sent_sem.at[len(sent)])


def settle(held_ref, out_ref, sem):
    copy = pltpu.make_async_copy(held_ref, out_ref, sem)
    copy.start()
    copy.wait()


def by_head(sections, chunks, pieces, stream, queries, keys, values, out_weight, gains):
    devices = lax.axis_size("ctx")
    rows, width = stream.shape
    query_width = queries.shape[2] // devices
    chunk_rows = rows // chunks
    piece_rows, count = chunk_rows // pieces, chunks * pieces
    half = (width // LANES + 1) // 2 * LANES
    chips = devices // 2
    narrow, wide = jnp.bfloat16, jnp.float32
    anywhere = pl.BlockSpec(memory_space=pltpu.HBM)
    in_vmem = pl.BlockSpec(memory_space=pltpu.VMEM)
    dma = pltpu.SemaphoreType.DMA
    out = pl.pallas_call(
        functools.partial(fused_kernel, sections, chunks, pieces, half),
        out_shape=pltpu.VMEM((count, piece_rows, width), narrow),
        in_specs=[anywhere] * 6,
        out_specs=in_vmem,
        scratch_shapes=[
            pltpu.VMEM((chunks, devices, chunk_rows, query_width), narrow),
            pltpu.VMEM((devices * rows, HEAD_WIDTH), narrow),
            pltpu.VMEM((devices * rows, HEAD_WIDTH), narrow),
            pltpu.VMEM((HEAD_WIDTH, devices * rows), narrow),
            pltpu.VMEM(out_weight.shape[1:], narrow),
            pltpu.VMEM(gains.shape, narrow),
            pltpu.VMEM((2, chunks, chips, chunk_rows, query_width), narrow),
            pltpu.VMEM((count, chips, piece_rows, width), narrow),
            pltpu.VMEM((count, chips, piece_rows, width), narrow),
            pltpu.VMEM((count, piece_rows, width), narrow),
            pltpu.VMEM((count, piece_rows, width), narrow),
            pltpu.VMEM((count, piece_rows, width), narrow),
            pltpu.VMEM((count, piece_rows, width), narrow),
            pltpu.VMEM((count, 2, piece_rows, width), narrow),
            pltpu.VMEM((count, chips, piece_rows, width), wide),
            pltpu.VMEM((count, piece_rows, width), wide),
            pltpu.VMEM((count, piece_rows, width), wide),
            pltpu.VMEM((count, piece_rows, width), narrow),
            dma((2,)),
            dma,
            dma((2,)),
            dma((chunks,)),
            dma((7,)),
            dma((min(chunks, 4),)),
            dma((min(count, 8),)),
            dma((count,)),
            dma((count + TAIL,)),
        ],
        compiler_params=pltpu.CompilerParams(
            collective_id=0, has_side_effects=True, vmem_limit_bytes=VMEM_GRANT
        ),
    )(gains, stream, queries[0], keys[0], values[0], out_weight[0])
    return pl.pallas_call(
        settle,
        out_shape=jax.ShapeDtypeStruct(out.shape, out.dtype),
        in_specs=[in_vmem],
        out_specs=anywhere,
        scratch_shapes=[dma(())],
        compiler_params=pltpu.CompilerParams(vmem_limit_bytes=2_000_000),
    )(out).reshape(1, rows, width)


def fits_by_head(mesh, rows):
    devices = mesh.shape["ctx"]
    return devices == KEY_HEADS and devices * rows <= WINDOW_LENGTH and devices % 8 == 0


def solution(mesh):
    in_specs = (
        P("ctx", None),
        P("section", "ctx", None),
        P("section", "ctx", None),
        P("section", "ctx", None),
        P("section", "ctx", None),
        P("section", None),
    )
    out_specs = P("section", "ctx", None)
    sections = mesh.shape["section"]

    def step(stream, *rest):
        rows = stream.shape[0]
        if fits_by_head(mesh, rows):
            return by_head(sections, CHUNKS, PIECES, stream, *rest)
        return local(stream, *rest)

    return jax.shard_map(step, mesh=mesh, in_specs=in_specs, out_specs=out_specs, check_vma=False)
```

```python
import functools
import math

import jax
import jax.numpy as jnp
from jax import lax
from jax.experimental import pallas as pl
from jax.experimental.pallas import tpu as pltpu
from jax.sharding import PartitionSpec as P

KEY_HEADS = 8
HEAD_WIDTH = 128
WINDOW_LENGTH = 1024
QUERY_SCALAR = 168
QUERY_PER_KEY = 2


norm_eps = 1e-06


def passed_along(block, axis, distance):
    devices = range(lax.axis_size(axis))
    route = [(i - distance, i) for i in devices if i - distance in devices]
    return lax.ppermute(block, axis, route)


def attend_block(query_matrix_rows, key_matrix_rows, value_matrix_rows, allowed, scale_factor):
    scores = (
        jnp.einsum(
            "qhgd,khd->hgqk", query_matrix_rows, key_matrix_rows, preferred_element_type=jnp.float32
        )
        * scale_factor
    )
    scores = jnp.where(allowed, scores, -jnp.inf)
    row_top = jnp.max(scores, axis=-1, keepdims=True)
    exponent = jnp.exp(scores - row_top)
    row_total = jnp.sum(exponent, axis=-1, keepdims=True)
    weights = exponent.astype(jnp.bfloat16)
    mixed_rows = jnp.einsum(
        "hgqk,khd->qhgd", weights, value_matrix_rows, preferred_element_type=jnp.float32
    )
    return mixed_rows / jnp.transpose(row_total, (2, 0, 1, 3))


def local(stream, queries, keys, values, out_weight, gains):
    tok_rows = stream.shape[0]
    span_rows = min(tok_rows, WINDOW_LENGTH)
    hop_count = WINDOW_LENGTH // span_rows
    own_tail = (keys[0, tok_rows - span_rows :], values[0, tok_rows - span_rows :])
    pieces = [
        passed_along((own_tail[0], own_tail[1]), "ctx", distance)
        for distance in range(hop_count, 0, -1)
    ]
    key_matrix_rows = jnp.concatenate([piece_pair[0] for piece_pair in pieces] + [keys[0]], axis=0)
    value_matrix_rows = jnp.concatenate(
        [piece_pair[1] for piece_pair in pieces] + [values[0]], axis=0
    )
    ctx_base = lax.axis_index("ctx") * tok_rows
    query_pos = ctx_base + jnp.arange(tok_rows, dtype=jnp.int32)
    key_pos = ctx_base - WINDOW_LENGTH + jnp.arange(WINDOW_LENGTH + tok_rows, dtype=jnp.int32)
    allowed = (
        (key_pos[None, :] >= 0)
        & (key_pos[None, :] <= query_pos[:, None])
        & (key_pos[None, :] > query_pos[:, None] - WINDOW_LENGTH)
    )
    scale_factor = QUERY_SCALAR ** (-0.5)
    heads_per_block = math.gcd(KEY_HEADS, 4)
    query_width = heads_per_block * QUERY_PER_KEY * HEAD_WIDTH
    key_width = heads_per_block * HEAD_WIDTH
    outputs_list = []
    for query_head_group in range(KEY_HEADS // heads_per_block):
        query_cols = queries[
            0, :, query_head_group * query_width : (query_head_group + 1) * query_width
        ].reshape(tok_rows, heads_per_block, QUERY_PER_KEY, HEAD_WIDTH)
        key_cols = key_matrix_rows[
            :, query_head_group * key_width : (query_head_group + 1) * key_width
        ].reshape(WINDOW_LENGTH + tok_rows, heads_per_block, HEAD_WIDTH)
        value_cols = value_matrix_rows[
            :, query_head_group * key_width : (query_head_group + 1) * key_width
        ].reshape(WINDOW_LENGTH + tok_rows, heads_per_block, HEAD_WIDTH)
        mixed_rows = attend_block(query_cols, key_cols, value_cols, allowed, scale_factor)
        outputs_list.append(mixed_rows.reshape(tok_rows, query_width))
    attended = jnp.concatenate(outputs_list, axis=1).astype(jnp.bfloat16)
    projected = jnp.dot(
        attended,
        lax.all_gather(out_weight[0], "ctx", axis=0, tiled=True),
        preferred_element_type=jnp.float32,
    )
    mean_square = jnp.mean(projected * projected, axis=-1, keepdims=True)
    branch = projected * lax.rsqrt(mean_square + norm_eps) * gains[0].astype(jnp.float32)
    section_index = lax.axis_index("section")
    section_count = lax.axis_size("section")
    running = jnp.where(
        section_index == 0, stream.astype(jnp.float32) + branch, jnp.zeros_like(branch)
    )
    for turn_index in range(section_count - 1):
        arrived = passed_along(running.astype(jnp.bfloat16), "section", 1).astype(running.dtype)
        running = jnp.where(section_index == turn_index + 1, arrived + branch, running)
    return running.astype(jnp.bfloat16)[None]


LANES = 128
MESH = pl.DeviceIdType.MESH
CHUNKS = 8
PIECES = 2
FIRST = 1
NEAR = 3
SECOND = 3
LAST = 6
HOP = 1
TAIL = 4
TILE = 512
VMEM_GRANT = 60_000_000


def column_tiles(start, stop, width):
    return [(at, min(at + width, stop) - at) for at in range(start, stop, width)]


def fused_kernel(
    sections,
    chunks,
    pieces,
    half,
    gains_hbm,
    stream_ref,
    q_ref,
    k_ref,
    v_ref,
    w_hbm,
    out_ref,
    qbuf,
    kbuf,
    vbuf,
    vturned,
    w_ref,
    gains_ref,
    att,
    pair_out,
    pair_in,
    far,
    first_in,
    near,
    onward,
    second_in,
    own,
    keep_me,
    keep,
    base,
    local_sem,
    key_sem,
    value_sem,
    query_sem,
    sent_sem,
    pair_sem,
    first_sem,
    second_sem,
    chain_sem,
):
    me = lax.axis_index("ctx")
    section = lax.axis_index("section")
    devices, chunk_rows, query_width = qbuf.shape[1:]
    width = w_ref.shape[1]
    rows = chunks * chunk_rows
    piece_rows = chunk_rows // pieces
    quarter, pair_count = devices // 4, devices // 2
    core = me % 2
    across = (me // quarter) % 2
    up = me // pair_count
    flips = (1 - 2 * core, quarter * (1 - 2 * across), pair_count * (1 - 2 * up))

    def peer(flip_core, flip_x, flip_y):
        return me + flips[0] * flip_core + flips[1] * flip_x + flips[2] * flip_y

    sibling, beside, above, diagonal = peer(1, 0, 0), peer(0, 1, 0), peer(0, 0, 1), peer(0, 1, 1)
    has_prev = jnp.minimum(section, 1)
    has_next = jnp.minimum(sections - 1 - section, 1)

    def own_rows(buf):
        return buf.at[pl.ds(pl.multiple_of(me * rows, rows), rows)]

    def head_columns(ref, who, span):
        return ref.at[:, pl.ds(pl.multiple_of(who * span, span), span)]

    tail_start = chunks * pieces - TAIL
    sides = ((0, half), (half, width))

    def hand_parts(late, piece):
        if late:
            return (sides[0], piece), (sides[1], piece + TAIL)
        return (((0, width), piece),)

    w_copy = pltpu.make_async_copy(w_hbm, w_ref, local_sem.at[0])
    w_copy.start()
    gains_copy = pltpu.make_async_copy(gains_hbm, gains_ref, local_sem.at[1])
    gains_copy.start()

    @pl.when(section == 0)
    def _():
        for piece in range(chunks * pieces):
            for (at, stop), landed in hand_parts(piece >= tail_start, piece):
                columns = pl.ds(at, stop - at)
                pltpu.make_async_copy(
                    stream_ref.at[pl.ds(piece * piece_rows, piece_rows), columns],
                    base.at[piece, :, columns],
                    chain_sem.at[landed],
                ).start()

    def query_part(who, chunk):
        source = q_ref.at[
            pl.ds(chunk * chunk_rows, chunk_rows),
            pl.ds(pl.multiple_of(who * query_width, query_width), query_width),
        ]
        return source, qbuf.at[chunk, me], sent_sem.at[2], query_sem.at[chunk]

    def blocks_for(who):
        key_block = head_columns(k_ref, who, HEAD_WIDTH), own_rows(kbuf), sent_sem.at[0], key_sem
        value_block = (
            head_columns(v_ref, who, HEAD_WIDTH),
            own_rows(vbuf),
            sent_sem.at[1],
            value_sem.at[me // pair_count],
        )
        asked = [query_part(who, chunk) for chunk in range(chunks)]
        return [key_block, asked[0], value_block] + asked[1:]

    for source, target, _, landed in blocks_for(me):
        pltpu.make_async_copy(source, target, landed).start()

    order = [(0, 1, 1), (1, 1, 1), (0, 1, 0), (0, 0, 1), (1, 1, 0), (1, 0, 1), (1, 0, 0)]
    barrier = pltpu.get_barrier_semaphore()
    for flip in order:
        pl.semaphore_signal(barrier, inc=1, device_id=(section, peer(*flip)), device_id_type=MESH)

    @pl.when(section > 0)
    def _():
        pl.semaphore_signal(barrier, inc=1, device_id=(section - 1, me), device_id_type=MESH)

    @pl.when(section < sections - 1)
    def _():
        pl.semaphore_signal(barrier, inc=1, device_id=(section + 1, me), device_id_type=MESH)

    pl.semaphore_wait(barrier, len(order) + has_prev + has_next)

    def exchange(who):
        return [
            pltpu.make_async_remote_copy(
                src_ref=source,
                dst_ref=target,
                send_sem=sent,
                recv_sem=landed,
                device_id=(section, who),
                device_id_type=MESH,
            )
            for source, target, sent, landed in blocks_for(who)
        ]

    for wave in zip(*[exchange(peer(*flip)) for flip in order]):
        for copy in wave:
            copy.start()

    def arrive(target, sem):
        pltpu.make_async_copy(target, target, sem).wait()

    narrow = jnp.bfloat16
    factor = QUERY_SCALAR ** (-0.5) * math.log2(math.e)
    group = query_width // HEAD_WIDTH
    asks = devices * group * chunk_rows
    low_asks, low_keys = asks // 2, devices * rows // 2

    def column_positions(chunk):
        lane = lax.broadcasted_iota(jnp.int32, (1, asks), 1)
        block = lane // (group * chunk_rows)
        return block * rows + chunk * chunk_rows + lane % chunk_rows

    def visible(scores, first_key, positions):
        key = lax.broadcasted_iota(jnp.int32, scores.shape, 0) + first_key
        return jnp.where(key <= positions, scores, -jnp.inf)

    def score(key_rows, query_rows):
        return lax.dot_general(
            key_rows, query_rows, (((1,), (1,)), ((), ())), preferred_element_type=jnp.float32
        )

    def turn_values():
        for side in range(2):
            span = pl.ds(side * low_keys, low_keys)
            arrive(vbuf.at[span], value_sem.at[side])
            vturned[:, side * low_keys : (side + 1) * low_keys] = vbuf[span].T

    def weigh(chunk):
        arrive(qbuf.at[chunk], query_sem.at[chunk])
        asked = jnp.concatenate(
            [
                qbuf[chunk, block, :, head * HEAD_WIDTH : (head + 1) * HEAD_WIDTH]
                for block in range(devices)
                for head in range(group)
            ],
            axis=0,
        )
        positions = column_positions(chunk)
        early = score(kbuf[:low_keys], asked)
        late = score(kbuf[low_keys:], asked[low_asks:])
        left = visible(early[:, :low_asks], 0, positions[:, :low_asks])
        right = early[:, low_asks:]
        late = visible(late, low_keys, positions[:, low_asks:])
        left_top = jnp.max(left, axis=0, keepdims=True)
        right_top = jnp.maximum(
            jnp.max(right, axis=0, keepdims=True), jnp.max(late, axis=0, keepdims=True)
        )
        left = jnp.exp2((left - left_top) * factor)
        right = jnp.exp2((right - right_top) * factor)
        late = jnp.exp2((late - right_top) * factor)
        left_total = jnp.sum(left, axis=0, keepdims=True)
        right_total = jnp.sum(right, axis=0, keepdims=True) + jnp.sum(late, axis=0, keepdims=True)
        early = jnp.concatenate([left.astype(narrow), right.astype(narrow)], axis=1)
        return early, late.astype(narrow), left_total, right_total

    def mix(chunk, early, late, left_total, right_total):
        mixed = jnp.dot(vturned[:, :low_keys], early, preferred_element_type=jnp.float32)
        mixed_late = jnp.dot(vturned[:, low_keys:], late, preferred_element_type=jnp.float32)
        halves = (
            mixed[:, :low_asks] / left_total,
            (mixed[:, low_asks:] + mixed_late) / right_total,
        )
        for index, part in enumerate(halves):
            turned = part.T.astype(narrow)
            for within in range(devices // 2):
                block = index * (devices // 2) + within
                for head in range(group):
                    start = (within * group + head) * chunk_rows
                    att[
                        block % 2,
                        chunk,
                        block // 2,
                        :,
                        head * HEAD_WIDTH : (head + 1) * HEAD_WIDTH,
                    ] = turned[start : start + chunk_rows]

    def remote(source, target, sent, landed, who):
        return pltpu.make_async_remote_copy(
            src_ref=source,
            dst_ref=target,
            send_sem=sent,
            recv_sem=landed,
            device_id=who,
            device_id_type=MESH,
        )

    def pair_copy(chunk):
        span = pl.ds(chunk * pieces, pieces)
        landed = pair_sem.at[chunk % pair_sem.shape[0]]
        return remote(
            pair_out.at[span], pair_in.at[span], sent_sem.at[3], landed, (section, sibling)
        )

    def for_each_way(piece, send):
        for odd in range(2):

            @pl.when(piece % 2 == odd)
            def _():
                send(sides[odd], sides[1 - odd])

    def first_copies(piece):
        landed = first_sem.at[piece % first_sem.shape[0]]

        def send(by_x, by_y):
            for (at, stop), who in ((by_x, beside), (by_y, above)):
                part = piece, slice(None), pl.ds(at, stop - at)
                remote(
                    far.at[part], first_in.at[part], sent_sem.at[4], landed, (section, who)
                ).start()

        for_each_way(piece, send)

    def second_copies(piece, which, by_x, by_y):
        for (at, stop), who in ((by_x, beside), (by_y, above)):
            columns = pl.ds(at, stop - at)
            remote(
                (near, onward)[which].at[piece, :, columns],
                second_in.at[piece, which, :, columns],
                sent_sem.at[5],
                second_sem.at[piece],
                (section, who),
            ).start()

    chip_count = pair_count
    places = [who // 2 for who in (beside, diagonal, above, me)]

    def product(chunk):
        theirs = chip_count * chunk_rows
        left = jnp.concatenate(
            [att[1 - core, chunk].reshape(theirs, query_width)]
            + [att[core, chunk, place] for place in places],
            axis=0,
        )
        for at, span in column_tiles(0, width, TILE):
            part = jnp.dot(left, w_ref[:, at : at + span], preferred_element_type=jnp.float32)
            part = part.reshape(2, chip_count, pieces, piece_rows, span)
            for index in range(pieces):
                piece = chunk * pieces + index
                pair_out[piece, :, :, at : at + span] = part[0, :, index].astype(narrow)
                own[piece, :, :, at : at + span] = part[1, :, index]
        pair_copy(chunk).start()

    def summed(piece, index, at, stop):
        return own[piece, index, :, at:stop] + pair_in[piece, places[index], :, at:stop].astype(
            jnp.float32
        )

    def send_far(piece):
        chunk = piece // pieces

        @pl.when(piece % pieces == 0)
        def _():
            span = pl.ds(chunk * pieces, pieces)
            arrive(pair_in.at[span], pair_sem.at[chunk % pair_sem.shape[0]])

        far[piece] = summed(piece, 1, 0, width).astype(narrow)
        first_copies(piece)

    def send_near(piece):
        def send(by_x, by_y):
            near[piece, :, by_x[0] : by_x[1]] = summed(piece, 0, *by_x).astype(narrow)
            near[piece, :, by_y[0] : by_y[1]] = summed(piece, 2, *by_y).astype(narrow)
            second_copies(piece, 0, by_x, by_y)
            keep[piece, :, by_x[0] : by_x[1]] = summed(piece, 2, *by_x)
            keep[piece, :, by_y[0] : by_y[1]] = summed(piece, 0, *by_y)

        for_each_way(piece, send)
        keep_me[piece] = summed(piece, 3, 0, width)

    def second_turn(piece):
        arrive(first_in.at[piece], first_sem.at[piece % first_sem.shape[0]])
        onward[piece] = (keep[piece] + first_in[piece].astype(jnp.float32)).astype(narrow)
        for_each_way(piece, lambda by_x, by_y: second_copies(piece, 1, by_y, by_x))

    def normalise(piece):
        arrive(second_in.at[piece], second_sem.at[piece])
        received = second_in[piece].astype(jnp.float32)
        full = keep_me[piece] + received[0] + received[1]
        squares = jnp.sum(full * full, axis=1, keepdims=True)
        ratio = lax.rsqrt(squares * (1.0 / width) + norm_eps)
        keep_me[piece] = full * ratio * gains_ref[...].astype(jnp.float32)

    onward_device = (jnp.minimum(section + 1, sections - 1), me)

    def hand_parts_on(late, piece):
        for (at, stop), landed in hand_parts(late, piece):
            part = piece, slice(None), pl.ds(at, stop - at)
            arrive(base.at[part], chain_sem.at[landed])
            added = base[piece, :, at:stop].astype(jnp.float32) + keep_me[piece, :, at:stop]
            out_ref[piece, :, at:stop] = added.astype(out_ref.dtype)

            @pl.when(section < sections - 1)
            def _():
                remote(
                    out_ref.at[part],
                    base.at[part],
                    sent_sem.at[6],
                    chain_sem.at[landed],
                    onward_device,
                ).start()

    def hand_on(piece):
        @pl.when(piece < tail_start)
        def _():
            hand_parts_on(False, piece)

        @pl.when(piece >= tail_start)
        def _():
            hand_parts_on(True, piece)

    arrive(kbuf, key_sem)
    weights = weigh(0)
    turn_values()
    mix(0, *weights)
    w_copy.wait()
    gains_copy.wait()
    product(0)
    mix(1, *weigh(1))
    product(1)

    count = chunks * pieces

    def turn(step, carry):
        def staged(lag, stage):
            piece = step - lag

            @pl.when((piece >= 0) & (piece < chunks * pieces))
            def _():
                stage(piece)

        ahead = step - FIRST

        @pl.when((ahead % pieces == 0) & (ahead >= 0) & (ahead < count))
        def _():
            for index in range(pieces):
                send_far(ahead + index)

        staged(NEAR, send_near)
        chunk = step // pieces + 2

        @pl.when((step % pieces == pieces - 1) & (chunk < chunks))
        def _():
            mix(chunk, *weigh(chunk))
            product(chunk)

        staged(SECOND, second_turn)
        staged(LAST, normalise)
        staged(LAST + HOP * section, hand_on)
        return carry

    lax.fori_loop(0, chunks * pieces + LAST + HOP * (sections - 1), turn, 0)

    sent = (
        kbuf.at[pl.ds(0, (devices - 1) * rows)],
        vbuf.at[pl.ds(0, (devices - 1) * rows)],
        qbuf.at[:, pl.ds(0, devices - 1)],
        pair_out,
        first_in,
        second_in,
    )
    for index, source in enumerate(sent):
        arrive(source, sent_sem.at[index])

    @pl.when(section < sections - 1)
    def _():
        arrive(out_ref, sent_sem.at[len(sent)])


def settle(held_ref, out_ref, sem):
    copy = pltpu.make_async_copy(held_ref, out_ref, sem)
    copy.start()
    copy.wait()


def by_head(sections, chunks, pieces, stream, queries, keys, values, out_weight, gains):
    devices = lax.axis_size("ctx")
    rows, width = stream.shape
    query_width = queries.shape[2] // devices
    chunk_rows = rows // chunks
    piece_rows, count = chunk_rows // pieces, chunks * pieces
    half = (width // LANES + 1) // 2 * LANES
    chips = devices // 2
    narrow, wide = jnp.bfloat16, jnp.float32
    anywhere = pl.BlockSpec(memory_space=pltpu.HBM)
    in_vmem = pl.BlockSpec(memory_space=pltpu.VMEM)
    dma = pltpu.SemaphoreType.DMA
    out = pl.pallas_call(
        functools.partial(fused_kernel, sections, chunks, pieces, half),
        out_shape=pltpu.VMEM((count, piece_rows, width), narrow),
        in_specs=[anywhere] * 6,
        out_specs=in_vmem,
        scratch_shapes=[
            pltpu.VMEM((chunks, devices, chunk_rows, query_width), narrow),
            pltpu.VMEM((devices * rows, HEAD_WIDTH), narrow),
            pltpu.VMEM((devices * rows, HEAD_WIDTH), narrow),
            pltpu.VMEM((HEAD_WIDTH, devices * rows), narrow),
            pltpu.VMEM(out_weight.shape[1:], narrow),
            pltpu.VMEM(gains.shape, narrow),
            pltpu.VMEM((2, chunks, chips, chunk_rows, query_width), narrow),
            pltpu.VMEM((count, chips, piece_rows, width), narrow),
            pltpu.VMEM((count, chips, piece_rows, width), narrow),
            pltpu.VMEM((count, piece_rows, width), narrow),
            pltpu.VMEM((count, piece_rows, width), narrow),
            pltpu.VMEM((count, piece_rows, width), narrow),
            pltpu.VMEM((count, piece_rows, width), narrow),
            pltpu.VMEM((count, 2, piece_rows, width), narrow),
            pltpu.VMEM((count, chips, piece_rows, width), wide),
            pltpu.VMEM((count, piece_rows, width), wide),
            pltpu.VMEM((count, piece_rows, width), wide),
            pltpu.VMEM((count, piece_rows, width), narrow),
            dma((2,)),
            dma,
            dma((2,)),
            dma((chunks,)),
            dma((7,)),
            dma((min(chunks, 4),)),
            dma((min(count, 8),)),
            dma((count,)),
            dma((count + TAIL,)),
        ],
        compiler_params=pltpu.CompilerParams(
            collective_id=0, has_side_effects=True, vmem_limit_bytes=VMEM_GRANT
        ),
    )(gains, stream, queries[0], keys[0], values[0], out_weight[0])
    return pl.pallas_call(
        settle,
        out_shape=jax.ShapeDtypeStruct(out.shape, out.dtype),
        in_specs=[in_vmem],
        out_specs=anywhere,
        scratch_shapes=[dma(())],
        compiler_params=pltpu.CompilerParams(vmem_limit_bytes=2_000_000),
    )(out).reshape(1, rows, width)


def fits_by_head(mesh, rows):
    devices = mesh.shape["ctx"]
    return devices == KEY_HEADS and devices * rows <= WINDOW_LENGTH and devices % 8 == 0


def solution(mesh):
    in_specs = (
        P("ctx", None),
        P("section", "ctx", None),
        P("section", "ctx", None),
        P("section", "ctx", None),
        P("section", "ctx", None),
        P("section", None),
    )
    out_specs = P("section", "ctx", None)
    sections = mesh.shape["section"]

    def step(stream, *rest):
        rows = stream.shape[0]
        if fits_by_head(mesh, rows):
            return by_head(sections, CHUNKS, PIECES, stream, *rest)
        return local(stream, *rest)

    return jax.shard_map(step, mesh=mesh, in_specs=in_specs, out_specs=out_specs, check_vma=False)
```

```python
import functools
import math

import jax
import jax.numpy as jnp
from jax import lax
from jax.experimental import pallas as pl
from jax.experimental.pallas import tpu as pltpu
from jax.sharding import PartitionSpec as P

KEY_HEADS = 8
HEAD_WIDTH = 128
WINDOW_LENGTH = 1024
QUERY_SCALAR = 168
QUERY_PER_KEY = 2


norm_eps = 1e-06


def passed_along(block, axis, distance):
    devices = range(lax.axis_size(axis))
    route = [(i - distance, i) for i in devices if i - distance in devices]
    return lax.ppermute(block, axis, route)


def attend_block(query_matrix_rows, key_matrix_rows, value_matrix_rows, allowed, scale_factor):
    scores = (
        jnp.einsum(
            "qhgd,khd->hgqk", query_matrix_rows, key_matrix_rows, preferred_element_type=jnp.float32
        )
        * scale_factor
    )
    scores = jnp.where(allowed, scores, -jnp.inf)
    row_top = jnp.max(scores, axis=-1, keepdims=True)
    exponent = jnp.exp(scores - row_top)
    row_total = jnp.sum(exponent, axis=-1, keepdims=True)
    weights = exponent.astype(jnp.bfloat16)
    mixed_rows = jnp.einsum(
        "hgqk,khd->qhgd", weights, value_matrix_rows, preferred_element_type=jnp.float32
    )
    return mixed_rows / jnp.transpose(row_total, (2, 0, 1, 3))


def local(stream, queries, keys, values, out_weight, gains):
    tok_rows = stream.shape[0]
    span_rows = min(tok_rows, WINDOW_LENGTH)
    hop_count = WINDOW_LENGTH // span_rows
    own_tail = (keys[0, tok_rows - span_rows :], values[0, tok_rows - span_rows :])
    pieces = [
        passed_along((own_tail[0], own_tail[1]), "ctx", distance)
        for distance in range(hop_count, 0, -1)
    ]
    key_matrix_rows = jnp.concatenate([piece_pair[0] for piece_pair in pieces] + [keys[0]], axis=0)
    value_matrix_rows = jnp.concatenate(
        [piece_pair[1] for piece_pair in pieces] + [values[0]], axis=0
    )
    ctx_base = lax.axis_index("ctx") * tok_rows
    query_pos = ctx_base + jnp.arange(tok_rows, dtype=jnp.int32)
    key_pos = ctx_base - WINDOW_LENGTH + jnp.arange(WINDOW_LENGTH + tok_rows, dtype=jnp.int32)
    allowed = (
        (key_pos[None, :] >= 0)
        & (key_pos[None, :] <= query_pos[:, None])
        & (key_pos[None, :] > query_pos[:, None] - WINDOW_LENGTH)
    )
    scale_factor = QUERY_SCALAR ** (-0.5)
    heads_per_block = math.gcd(KEY_HEADS, 4)
    query_width = heads_per_block * QUERY_PER_KEY * HEAD_WIDTH
    key_width = heads_per_block * HEAD_WIDTH
    outputs_list = []
    for query_head_group in range(KEY_HEADS // heads_per_block):
        query_cols = queries[
            0, :, query_head_group * query_width : (query_head_group + 1) * query_width
        ].reshape(tok_rows, heads_per_block, QUERY_PER_KEY, HEAD_WIDTH)
        key_cols = key_matrix_rows[
            :, query_head_group * key_width : (query_head_group + 1) * key_width
        ].reshape(WINDOW_LENGTH + tok_rows, heads_per_block, HEAD_WIDTH)
        value_cols = value_matrix_rows[
            :, query_head_group * key_width : (query_head_group + 1) * key_width
        ].reshape(WINDOW_LENGTH + tok_rows, heads_per_block, HEAD_WIDTH)
        mixed_rows = attend_block(query_cols, key_cols, value_cols, allowed, scale_factor)
        outputs_list.append(mixed_rows.reshape(tok_rows, query_width))
    attended = jnp.concatenate(outputs_list, axis=1).astype(jnp.bfloat16)
    projected = jnp.dot(
        attended,
        lax.all_gather(out_weight[0], "ctx", axis=0, tiled=True),
        preferred_element_type=jnp.float32,
    )
    mean_square = jnp.mean(projected * projected, axis=-1, keepdims=True)
    branch = projected * lax.rsqrt(mean_square + norm_eps) * gains[0].astype(jnp.float32)
    section_index = lax.axis_index("section")
    section_count = lax.axis_size("section")
    running = jnp.where(
        section_index == 0, stream.astype(jnp.float32) + branch, jnp.zeros_like(branch)
    )
    for turn_index in range(section_count - 1):
        arrived = passed_along(running.astype(jnp.bfloat16), "section", 1).astype(running.dtype)
        running = jnp.where(section_index == turn_index + 1, arrived + branch, running)
    return running.astype(jnp.bfloat16)[None]


LANES = 128
MESH = pl.DeviceIdType.MESH
CHUNKS = 8
PIECES = 2
FIRST = 1
NEAR = 3
SECOND = 3
LAST = 6
HOP = 1
TAIL = 5
HAND = 3
TILE = 512
VMEM_GRANT = 60_000_000


def column_tiles(start, stop, width):
    return [(at, min(at + width, stop) - at) for at in range(start, stop, width)]


def fused_kernel(
    sections,
    chunks,
    pieces,
    half,
    gains_hbm,
    stream_ref,
    q_ref,
    k_ref,
    v_ref,
    w_hbm,
    out_ref,
    qbuf,
    kbuf,
    vbuf,
    vturned,
    w_ref,
    gains_ref,
    att,
    pair_out,
    pair_in,
    far,
    first_in,
    near,
    onward,
    second_in,
    own,
    keep_me,
    keep,
    base,
    local_sem,
    key_sem,
    value_sem,
    query_sem,
    sent_sem,
    pair_sem,
    first_sem,
    second_sem,
    chain_sem,
):
    me = lax.axis_index("ctx")
    section = lax.axis_index("section")
    devices, chunk_rows, query_width = qbuf.shape[1:]
    width = w_ref.shape[1]
    rows = chunks * chunk_rows
    piece_rows = chunk_rows // pieces
    quarter, pair_count = devices // 4, devices // 2
    core = me % 2
    across = (me // quarter) % 2
    up = me // pair_count
    flips = (1 - 2 * core, quarter * (1 - 2 * across), pair_count * (1 - 2 * up))

    def peer(flip_core, flip_x, flip_y):
        return me + flips[0] * flip_core + flips[1] * flip_x + flips[2] * flip_y

    sibling, beside, above, diagonal = peer(1, 0, 0), peer(0, 1, 0), peer(0, 0, 1), peer(0, 1, 1)
    has_prev = jnp.minimum(section, 1)
    has_next = jnp.minimum(sections - 1 - section, 1)

    def own_rows(buf):
        return buf.at[pl.ds(pl.multiple_of(me * rows, rows), rows)]

    def head_columns(ref, who, span):
        return ref.at[:, pl.ds(pl.multiple_of(who * span, span), span)]

    tail_start = chunks * pieces - TAIL
    sides = ((0, half), (half, width))

    def hand_parts(late, piece):
        if late:
            edges = [width // LANES * part // HAND * LANES for part in range(HAND + 1)]
            return tuple(
                (edges[part : part + 2], piece + part * TAIL) for part in range(HAND)
            )
        return (((0, width), piece),)

    w_copy = pltpu.make_async_copy(w_hbm, w_ref, local_sem.at[0])
    w_copy.start()
    gains_copy = pltpu.make_async_copy(gains_hbm, gains_ref, local_sem.at[1])
    gains_copy.start()

    @pl.when(section == 0)
    def _():
        for piece in range(chunks * pieces):
            for (at, stop), landed in hand_parts(piece >= tail_start, piece):
                columns = pl.ds(at, stop - at)
                pltpu.make_async_copy(
                    stream_ref.at[pl.ds(piece * piece_rows, piece_rows), columns],
                    base.at[piece, :, columns],
                    chain_sem.at[landed],
                ).start()

    def query_part(who, chunk):
        source = q_ref.at[
            pl.ds(chunk * chunk_rows, chunk_rows),
            pl.ds(pl.multiple_of(who * query_width, query_width), query_width),
        ]
        return source, qbuf.at[chunk, me], sent_sem.at[2], query_sem.at[chunk]

    def blocks_for(who):
        key_block = head_columns(k_ref, who, HEAD_WIDTH), own_rows(kbuf), sent_sem.at[0], key_sem
        value_block = (
            head_columns(v_ref, who, HEAD_WIDTH),
            own_rows(vbuf),
            sent_sem.at[1],
            value_sem.at[me // pair_count],
        )
        asked = [query_part(who, chunk) for chunk in range(chunks)]
        return [key_block, asked[0], value_block] + asked[1:]

    for source, target, _, landed in blocks_for(me):
        pltpu.make_async_copy(source, target, landed).start()

    order = [(0, 1, 1), (1, 1, 1), (0, 1, 0), (0, 0, 1), (1, 1, 0), (1, 0, 1), (1, 0, 0)]
    barrier = pltpu.get_barrier_semaphore()
    for flip in order:
        pl.semaphore_signal(barrier, inc=1, device_id=(section, peer(*flip)), device_id_type=MESH)

    @pl.when(section > 0)
    def _():
        pl.semaphore_signal(barrier, inc=1, device_id=(section - 1, me), device_id_type=MESH)

    @pl.when(section < sections - 1)
    def _():
        pl.semaphore_signal(barrier, inc=1, device_id=(section + 1, me), device_id_type=MESH)

    pl.semaphore_wait(barrier, len(order) + has_prev + has_next)

    def exchange(who):
        return [
            pltpu.make_async_remote_copy(
                src_ref=source,
                dst_ref=target,
                send_sem=sent,
                recv_sem=landed,
                device_id=(section, who),
                device_id_type=MESH,
            )
            for source, target, sent, landed in blocks_for(who)
        ]

    for wave in zip(*[exchange(peer(*flip)) for flip in order]):
        for copy in wave:
            copy.start()

    def arrive(target, sem):
        pltpu.make_async_copy(target, target, sem).wait()

    narrow = jnp.bfloat16
    factor = QUERY_SCALAR ** (-0.5) * math.log2(math.e)
    group = query_width // HEAD_WIDTH
    asks = devices * group * chunk_rows
    low_asks, low_keys = asks // 2, devices * rows // 2

    def column_positions(chunk):
        lane = lax.broadcasted_iota(jnp.int32, (1, asks), 1)
        block = lane // (group * chunk_rows)
        return block * rows + chunk * chunk_rows + lane % chunk_rows

    def visible(scores, first_key, positions):
        key = lax.broadcasted_iota(jnp.int32, scores.shape, 0) + first_key
        return jnp.where(key <= positions, scores, -jnp.inf)

    def score(key_rows, query_rows):
        return lax.dot_general(
            key_rows, query_rows, (((1,), (1,)), ((), ())), preferred_element_type=jnp.float32
        )

    def turn_values():
        for side in range(2):
            span = pl.ds(side * low_keys, low_keys)
            arrive(vbuf.at[span], value_sem.at[side])
            vturned[:, side * low_keys : (side + 1) * low_keys] = vbuf[span].T

    def weigh(chunk):
        arrive(qbuf.at[chunk], query_sem.at[chunk])
        asked = jnp.concatenate(
            [
                qbuf[chunk, block, :, head * HEAD_WIDTH : (head + 1) * HEAD_WIDTH]
                for block in range(devices)
                for head in range(group)
            ],
            axis=0,
        )
        positions = column_positions(chunk)
        early = score(kbuf[:low_keys], asked)
        late = score(kbuf[low_keys:], asked[low_asks:])
        left = visible(early[:, :low_asks], 0, positions[:, :low_asks])
        right = early[:, low_asks:]
        late = visible(late, low_keys, positions[:, low_asks:])
        left_top = jnp.max(left, axis=0, keepdims=True)
        right_top = jnp.maximum(
            jnp.max(right, axis=0, keepdims=True), jnp.max(late, axis=0, keepdims=True)
        )
        left = jnp.exp2((left - left_top) * factor)
        right = jnp.exp2((right - right_top) * factor)
        late = jnp.exp2((late - right_top) * factor)
        left_total = jnp.sum(left, axis=0, keepdims=True)
        right_total = jnp.sum(right, axis=0, keepdims=True) + jnp.sum(late, axis=0, keepdims=True)
        early = jnp.concatenate([left.astype(narrow), right.astype(narrow)], axis=1)
        return early, late.astype(narrow), left_total, right_total

    def mix(chunk, early, late, left_total, right_total):
        mixed = jnp.dot(vturned[:, :low_keys], early, preferred_element_type=jnp.float32)
        mixed_late = jnp.dot(vturned[:, low_keys:], late, preferred_element_type=jnp.float32)
        halves = (
            mixed[:, :low_asks] / left_total,
            (mixed[:, low_asks:] + mixed_late) / right_total,
        )
        for index, part in enumerate(halves):
            turned = part.T.astype(narrow)
            for within in range(devices // 2):
                block = index * (devices // 2) + within
                for head in range(group):
                    start = (within * group + head) * chunk_rows
                    att[
                        block % 2,
                        chunk,
                        block // 2,
                        :,
                        head * HEAD_WIDTH : (head + 1) * HEAD_WIDTH,
                    ] = turned[start : start + chunk_rows]

    def remote(source, target, sent, landed, who):
        return pltpu.make_async_remote_copy(
            src_ref=source,
            dst_ref=target,
            send_sem=sent,
            recv_sem=landed,
            device_id=who,
            device_id_type=MESH,
        )

    def pair_copy(chunk):
        span = pl.ds(chunk * pieces, pieces)
        landed = pair_sem.at[chunk % pair_sem.shape[0]]
        return remote(
            pair_out.at[span], pair_in.at[span], sent_sem.at[3], landed, (section, sibling)
        )

    def for_each_way(piece, send):
        for odd in range(2):

            @pl.when(piece % 2 == odd)
            def _():
                send(sides[odd], sides[1 - odd])

    def first_copies(piece):
        landed = first_sem.at[piece % first_sem.shape[0]]

        def send(by_x, by_y):
            for (at, stop), who in ((by_x, beside), (by_y, above)):
                part = piece, slice(None), pl.ds(at, stop - at)
                remote(
                    far.at[part], first_in.at[part], sent_sem.at[4], landed, (section, who)
                ).start()

        for_each_way(piece, send)

    def second_copies(piece, which, by_x, by_y):
        for (at, stop), who in ((by_x, beside), (by_y, above)):
            columns = pl.ds(at, stop - at)
            remote(
                (near, onward)[which].at[piece, :, columns],
                second_in.at[piece, which, :, columns],
                sent_sem.at[5],
                second_sem.at[piece % second_sem.shape[0]],
                (section, who),
            ).start()

    chip_count = pair_count
    places = [who // 2 for who in (beside, diagonal, above, me)]

    def product(chunk):
        theirs = chip_count * chunk_rows
        left = jnp.concatenate(
            [att[1 - core, chunk].reshape(theirs, query_width)]
            + [att[core, chunk, place] for place in places],
            axis=0,
        )
        for at, span in column_tiles(0, width, TILE):
            part = jnp.dot(left, w_ref[:, at : at + span], preferred_element_type=jnp.float32)
            part = part.reshape(2, chip_count, pieces, piece_rows, span)
            for index in range(pieces):
                piece = chunk * pieces + index
                pair_out[piece, :, :, at : at + span] = part[0, :, index].astype(narrow)
                own[piece, :, :, at : at + span] = part[1, :, index]
        pair_copy(chunk).start()

    def summed(piece, index, at, stop):
        return own[piece, index, :, at:stop] + pair_in[piece, places[index], :, at:stop].astype(
            jnp.float32
        )

    def send_far(piece):
        chunk = piece // pieces

        @pl.when(piece % pieces == 0)
        def _():
            span = pl.ds(chunk * pieces, pieces)
            arrive(pair_in.at[span], pair_sem.at[chunk % pair_sem.shape[0]])

        far[piece] = summed(piece, 1, 0, width).astype(narrow)
        first_copies(piece)

    def send_near(piece):
        def send(by_x, by_y):
            near[piece, :, by_x[0] : by_x[1]] = summed(piece, 0, *by_x).astype(narrow)
            near[piece, :, by_y[0] : by_y[1]] = summed(piece, 2, *by_y).astype(narrow)
            second_copies(piece, 0, by_x, by_y)
            keep[piece, :, by_x[0] : by_x[1]] = summed(piece, 2, *by_x)
            keep[piece, :, by_y[0] : by_y[1]] = summed(piece, 0, *by_y)

        for_each_way(piece, send)
        keep_me[piece] = summed(piece, 3, 0, width)

    def second_turn(piece):
        arrive(first_in.at[piece], first_sem.at[piece % first_sem.shape[0]])
        onward[piece] = (keep[piece] + first_in[piece].astype(jnp.float32)).astype(narrow)
        for_each_way(piece, lambda by_x, by_y: second_copies(piece, 1, by_y, by_x))

    def normalise(piece):
        arrive(second_in.at[piece], second_sem.at[piece % second_sem.shape[0]])
        received = second_in[piece].astype(jnp.float32)
        full = keep_me[piece] + received[0] + received[1]
        squares = jnp.sum(full * full, axis=1, keepdims=True)
        ratio = lax.rsqrt(squares * (1.0 / width) + norm_eps)
        keep_me[piece] = full * ratio * gains_ref[...].astype(jnp.float32)

    onward_device = (jnp.minimum(section + 1, sections - 1), me)

    def hand_parts_on(late, piece):
        for (at, stop), landed in hand_parts(late, piece):
            part = piece, slice(None), pl.ds(at, stop - at)
            arrive(base.at[part], chain_sem.at[landed])
            added = base[piece, :, at:stop].astype(jnp.float32) + keep_me[piece, :, at:stop]
            out_ref[piece, :, at:stop] = added.astype(out_ref.dtype)

            @pl.when(section < sections - 1)
            def _():
                remote(
                    out_ref.at[part],
                    base.at[part],
                    sent_sem.at[6],
                    chain_sem.at[landed],
                    onward_device,
                ).start()

    def hand_on(piece):
        @pl.when(piece < tail_start)
        def _():
            hand_parts_on(False, piece)

        @pl.when(piece >= tail_start)
        def _():
            hand_parts_on(True, piece)

    arrive(kbuf, key_sem)
    weights = weigh(0)
    turn_values()
    mix(0, *weights)
    w_copy.wait()
    gains_copy.wait()
    product(0)
    mix(1, *weigh(1))
    product(1)

    count = chunks * pieces

    def turn(step, carry):
        def staged(lag, stage):
            piece = step - lag

            @pl.when((piece >= 0) & (piece < chunks * pieces))
            def _():
                stage(piece)

        ahead = step - FIRST

        @pl.when((ahead % pieces == 0) & (ahead >= 0) & (ahead < count))
        def _():
            for index in range(pieces):
                send_far(ahead + index)

        staged(NEAR, send_near)
        chunk = step // pieces + 2

        @pl.when((step % pieces == pieces - 1) & (chunk < chunks))
        def _():
            mix(chunk, *weigh(chunk))
            product(chunk)

        staged(SECOND, second_turn)
        staged(LAST, normalise)
        staged(LAST + HOP * section, hand_on)
        return carry

    lax.fori_loop(0, chunks * pieces + LAST + HOP * (sections - 1), turn, 0)

    sent = (
        kbuf.at[pl.ds(0, (devices - 1) * rows)],
        vbuf.at[pl.ds(0, (devices - 1) * rows)],
        qbuf.at[:, pl.ds(0, devices - 1)],
        pair_out,
        first_in,
        second_in,
    )
    for index, source in enumerate(sent):
        arrive(source, sent_sem.at[index])

    @pl.when(section < sections - 1)
    def _():
        arrive(out_ref, sent_sem.at[len(sent)])


def settle(held_ref, out_ref, sem):
    copy = pltpu.make_async_copy(held_ref, out_ref, sem)
    copy.start()
    copy.wait()


def by_head(sections, chunks, pieces, stream, queries, keys, values, out_weight, gains):
    devices = lax.axis_size("ctx")
    rows, width = stream.shape
    query_width = queries.shape[2] // devices
    chunk_rows = rows // chunks
    piece_rows, count = chunk_rows // pieces, chunks * pieces
    half = (width // LANES + 1) // 2 * LANES
    chips = devices // 2
    narrow, wide = jnp.bfloat16, jnp.float32
    anywhere = pl.BlockSpec(memory_space=pltpu.HBM)
    in_vmem = pl.BlockSpec(memory_space=pltpu.VMEM)
    dma = pltpu.SemaphoreType.DMA
    out = pl.pallas_call(
        functools.partial(fused_kernel, sections, chunks, pieces, half),
        out_shape=pltpu.VMEM((count, piece_rows, width), narrow),
        in_specs=[anywhere] * 6,
        out_specs=in_vmem,
        scratch_shapes=[
            pltpu.VMEM((chunks, devices, chunk_rows, query_width), narrow),
            pltpu.VMEM((devices * rows, HEAD_WIDTH), narrow),
            pltpu.VMEM((devices * rows, HEAD_WIDTH), narrow),
            pltpu.VMEM((HEAD_WIDTH, devices * rows), narrow),
            pltpu.VMEM(out_weight.shape[1:], narrow),
            pltpu.VMEM(gains.shape, narrow),
            pltpu.VMEM((2, chunks, chips, chunk_rows, query_width), narrow),
            pltpu.VMEM((count, chips, piece_rows, width), narrow),
            pltpu.VMEM((count, chips, piece_rows, width), narrow),
            pltpu.VMEM((count, piece_rows, width), narrow),
            pltpu.VMEM((count, piece_rows, width), narrow),
            pltpu.VMEM((count, piece_rows, width), narrow),
            pltpu.VMEM((count, piece_rows, width), narrow),
            pltpu.VMEM((count, 2, piece_rows, width), narrow),
            pltpu.VMEM((count, chips, piece_rows, width), wide),
            pltpu.VMEM((count, piece_rows, width), wide),
            pltpu.VMEM((count, piece_rows, width), wide),
            pltpu.VMEM((count, piece_rows, width), narrow),
            dma((2,)),
            dma,
            dma((2,)),
            dma((chunks,)),
            dma((7,)),
            dma((min(chunks, 4),)),
            dma((min(count, 8),)),
            dma((min(count, 12),)),
            dma((count + (HAND - 1) * TAIL,)),
        ],
        compiler_params=pltpu.CompilerParams(
            collective_id=0, has_side_effects=True, vmem_limit_bytes=VMEM_GRANT
        ),
    )(gains, stream, queries[0], keys[0], values[0], out_weight[0])
    return pl.pallas_call(
        settle,
        out_shape=jax.ShapeDtypeStruct(out.shape, out.dtype),
        in_specs=[in_vmem],
        out_specs=anywhere,
        scratch_shapes=[dma(())],
        compiler_params=pltpu.CompilerParams(vmem_limit_bytes=2_000_000),
    )(out).reshape(1, rows, width)


def fits_by_head(mesh, rows):
    devices = mesh.shape["ctx"]
    return devices == KEY_HEADS and devices * rows <= WINDOW_LENGTH and devices % 8 == 0


def solution(mesh):
    in_specs = (
        P("ctx", None),
        P("section", "ctx", None),
        P("section", "ctx", None),
        P("section", "ctx", None),
        P("section", "ctx", None),
        P("section", None),
    )
    out_specs = P("section", "ctx", None)
    sections = mesh.shape["section"]

    def step(stream, *rest):
        rows = stream.shape[0]
        if fits_by_head(mesh, rows):
            return by_head(sections, CHUNKS, PIECES, stream, *rest)
        return local(stream, *rest)

    return jax.shard_map(step, mesh=mesh, in_specs=in_specs, out_specs=out_specs, check_vma=False)
```
